32 devices in a mesh: dp: 16 (over z, y, core), ctx: 2 (over x).
Axes of the slice: x: 2, y: 2, z: 4, core: 2. Of those that a mesh axis runs over, the one named last changes fastest.
Arguments:
- tokens: bfloat16 [32, 1024, 768], P('dp', 'ctx'), may hold values from -17 to 17
- segments: int32 [32, 1024], P('dp'), may hold values from 0 to 7, never falling along the last dimension, each value on 1 to 512 neighbouring positions
- cotangent: float32 [32, 1024, 768], P('dp', 'ctx'), may hold values from -6 to 6
- w_query: bfloat16 [768, 768], P(('dp', 'ctx')), may hold values from -0.21875 to 0.21875
- w_key: bfloat16 [768, 768], P(('dp', 'ctx')), may hold values from -0.21875 to 0.21875
- w_value: bfloat16 [768, 768], P(('dp', 'ctx')), may hold values from -0.21875 to 0.21875
- w_output: bfloat16 [768, 768], P(('dp', 'ctx')), may hold values from -1.75 to 1.75
- w_inner: bfloat16 [768, 3072], P(('dp', 'ctx')), may hold values from -0.21875 to 0.21875
- w_outer: bfloat16 [3072, 768], P(('dp', 'ctx')), may hold values from -0.109375 to 0.109375
- b_query: bfloat16 [768], P(('dp', 'ctx')), may hold values from -3 to 3
- b_value: bfloat16 [768], P(('dp', 'ctx')), may hold values from -3 to 3
- b_output: bfloat16 [768], P(('dp', 'ctx')), may hold values from -3 to 3
- gain_one: bfloat16 [768], P(('dp', 'ctx')), may hold values from 0.5 to 1.5
- shift_one: bfloat16 [768], P(('dp', 'ctx')), may hold values from -3 to 3
- b_inner: bfloat16 [3072], P(('dp', 'ctx')), may hold values from -3 to 3
- b_outer: bfloat16 [768], P(('dp', 'ctx')), may hold values from -3 to 3
- gain_two: bfloat16 [768], P(('dp', 'ctx')), may hold values from 0.5 to 1.5
- shift_two: bfloat16 [768], P(('dp', 'ctx')), may hold values from -3 to 3
Outputs:
- result: float32 [32, 1024, 768], P('dp', 'ctx')
- input_grad: float32 [32, 1024, 768], P('dp', 'ctx')
- grad_w_query: float32 [768, 768], P(('dp', 'ctx'))
- grad_w_key: float32 [768, 768], P(('dp', 'ctx'))
- grad_w_value: float32 [768, 768], P(('dp', 'ctx'))
- grad_w_output: float32 [768, 768], P(('dp', 'ctx'))
- grad_w_inner: float32 [768, 3072], P(('dp', 'ctx'))
- grad_w_outer: float32 [3072, 768], P(('dp', 'ctx'))
- grad_b_query: float32 [768], P(('dp', 'ctx'))
- grad_b_value: float32 [768], P(('dp', 'ctx'))
- grad_b_output: float32 [768], P(('dp', 'ctx'))
- grad_gain_one: float32 [768], P(('dp', 'ctx'))
- grad_shift_one: float32 [768], P(('dp', 'ctx'))
- grad_b_inner: float32 [3072], P(('dp', 'ctx'))
- grad_b_outer: float32 [768], P(('dp', 'ctx'))
- grad_gain_two: float32 [768], P(('dp', 'ctx'))
- grad_shift_two: float32 [768], P(('dp', 'ctx'))
The draws below stay inside these ranges and needn't reach their ends.
Inputs may be any that keep to these rules, and one draw needn't show every extreme that they name: `segments`: within a sequence the document numbers never fall; a document has 1 to 512 tokens.
All inputs are finite; a program needn't handle non-finite values.
Results may differ from the reference program's by a relative error of at most 0.013.
The reference program's roundings to bfloat16 on the way (of `activated`, `grad_context_low` and `grad_scores`) count: a program that leaves them out, or rounds other values in their place, can miss the bound.
Values may be sent and summed in bfloat16 or wider, within the bound.
No kernel may reach another device: no remote copies, remote signals or barrier semaphores. Data moves between devices by JAX's collectives and lax.ppermute only.
A program may use at most 320 MiB of HBM per device.

```python
import math
import jax
import jax.numpy as jnp
import numpy as np
from jax import lax

D = 768
HEADS = 12
FF = 3072
HEAD_DIM = 64
SEQ_LEN = 1024
DOCS = 8
DOC_MOST = 512
SEQS = 32


def draw_tokens(key, part):
    drawn = jax.random.normal(key, (SEQS, SEQ_LEN, D), jnp.float32)
    return jnp.clip(drawn, -6.0, 6.0).astype(jnp.bfloat16)


def shard_levels(own_key, extent, shards, smallest, largest):
    def one(axis_at, parts):
        steps = jax.random.uniform(jax.random.fold_in(jax.random.fold_in(own_key, 6), axis_at), (parts,), jnp.float32, smallest / len(shards), largest / len(shards))
        return jnp.repeat(jnp.exp(steps), extent[axis_at] // parts).reshape((-1,) + (1,) * (len(extent) - axis_at - 1))

    level = one(*shards[0])
    for cut in shards[1:]:
        level = level * one(*cut)
    return level


def profile(number_of, total, limit, slope):
    portions = [(1 << 20) // math.isqrt(rank ** slope) + 1 for rank in range(2, number_of + 1)]
    rest, counts = total - limit - (number_of - 1), [1] * (number_of - 1)
    while rest > 0:
        movable = [i for i in range(number_of - 1) if counts[i] < limit]
        whole, left = sum([portions[i] for i in movable]), rest
        for i in movable:
            more = min(limit - counts[i], max(1, left * portions[i] // whole), rest)
            counts[i] = counts[i] + more
            rest = rest - more
    return np.array([limit] + counts)


def uneven_parts(stream_key, count, total, limit, slope):
    if count == 2:
        one = jax.random.randint(stream_key, (), max(1, total - limit), min(limit, total - 1) + 1)
        return jnp.stack([one, total - one])
    lengths = jnp.asarray(profile(count, total, limit, slope), jnp.int32)
    twos = (count - 1) // 2
    donor, sink = lengths[1:1 + 2 * twos:2], lengths[2:2 + 2 * twos:2]
    margin = jnp.minimum(donor - 1, limit - sink)
    moved = jax.random.randint(jax.random.fold_in(stream_key, 1), (twos,), 0, 1 << 20) % (margin + 1)
    lengths = lengths.at[1:1 + 2 * twos:2].set(donor - moved).at[2:2 + 2 * twos:2].set(sink + moved)
    return lengths[jax.random.permutation(jax.random.fold_in(stream_key, 2), count)]


def noise(rng, dims, spread, most, shards=(), dtype=jnp.bfloat16):
    array = spread * jax.random.normal(rng, dims, jnp.float32)
    if shards:
        array = array * shard_levels(rng, dims, shards, -0.22, 0.18)
    return jnp.clip(array, -most, most).astype(dtype)


def setup_inputs(seed: int = 0) -> dict:
    key_of = jax.random.split(jax.random.key(seed), 19)
    return {
        "tokens": draw_tokens(jax.random.fold_in(key_of[18], 71), 0),
        "segments": jax.vmap(lambda own: jnp.searchsorted(jnp.cumsum(uneven_parts(own, DOCS, SEQ_LEN, DOC_MOST, 2)), jnp.arange(SEQ_LEN), side="right"))(jax.random.split(key_of[1], SEQS)).reshape((SEQS, SEQ_LEN)).astype(jnp.int32),
        "cotangent": noise(key_of[2], (SEQS, SEQ_LEN, D), 1.0, 6.0, ((0, 16), (1, 2)), jnp.float32),
        "w_query": noise(key_of[3], (D, D), D ** -0.5, 0.21875, ((0, 32),)),
        "w_key": noise(key_of[4], (D, D), D ** -0.5, 0.21875, ((0, 32),)),
        "w_value": noise(key_of[5], (D, D), D ** -0.5, 0.21875, ((0, 32),)),
        "w_output": noise(key_of[6], (D, D), (D // 64) ** -0.5, 1.75, ((0, 32),)),
        "w_inner": noise(key_of[7], (D, FF), D ** -0.5, 0.21875, ((0, 32),)),
        "w_outer": noise(key_of[8], (FF, D), FF ** -0.5, 0.109375, ((0, 32),)),
        "b_query": noise(key_of[9], (D,), 0.5, 3.0, ((0, 32),)),
        "b_value": noise(key_of[10], (D,), 0.5, 3.0, ((0, 32),)),
        "b_output": noise(key_of[11], (D,), 0.5, 3.0, ((0, 32),)),
        "gain_one": jnp.clip(1.0 + 0.1 * jax.random.normal(key_of[12], (D,), jnp.float32), 0.5, 1.5).astype(jnp.bfloat16),
        "shift_one": noise(key_of[13], (D,), 0.5, 3.0, ((0, 32),)),
        "b_inner": noise(key_of[14], (FF,), 0.5, 3.0, ((0, 32),)),
        "b_outer": noise(key_of[15], (D,), 0.5, 3.0, ((0, 32),)),
        "gain_two": jnp.clip(1.0 + 0.1 * jax.random.normal(key_of[16], (D,), jnp.float32), 0.5, 1.5).astype(jnp.bfloat16),
        "shift_two": noise(key_of[17], (D,), 0.5, 3.0, ((0, 32),)),
    }


EPSILON = 1e-12
MASKED_SCORE = -1e+30

def product(left_side, right_side):
    return jnp.dot(left_side, right_side, preferred_element_type=jnp.float32)

def times_transposed(left_side, right_side):
    return lax.dot_general(left_side, right_side, (((1,), (1,)), ((), ())), preferred_element_type=jnp.float32)

def transposed_times(left_side, right_side):
    return lax.dot_general(left_side, right_side, (((0,), (0,)), ((), ())), preferred_element_type=jnp.float32)

def layer_norm(summed, gain_vec, shift_vec):
    row_mean = lax.optimization_barrier(jnp.mean(summed, -1, keepdims=True))
    centred = summed - row_mean
    variance = lax.optimization_barrier(jnp.mean(centred * centred, -1, keepdims=True))
    inv_std = lax.rsqrt(variance + EPSILON)
    normed = centred * inv_std
    return (normed * gain_vec.astype(jnp.float32) + shift_vec.astype(jnp.float32), normed, inv_std)

def norm_back(upstream, normed, inv_std, gain_vec):
    scaled_grad = upstream * gain_vec.astype(jnp.float32)
    first_term = lax.optimization_barrier(jnp.mean(scaled_grad, -1, keepdims=True))
    second_term = lax.optimization_barrier(jnp.mean(scaled_grad * normed, -1, keepdims=True))
    return inv_std * (scaled_grad - first_term - normed * second_term)

def normal_parts(inner_pre):
    normal_cdf = 0.5 * (1.0 + lax.erf(inner_pre * 0.7071067811865476))
    normal_pdf = jnp.exp(-0.5 * inner_pre * inner_pre) * 0.3989422804014327
    return (normal_cdf, normal_pdf)

def masked_scores(queries, keys_all, same_doc):
    scores = jnp.einsum('qhe,khe->hqk', queries.astype(jnp.float32), keys_all.astype(jnp.float32)) * HEAD_DIM ** (-0.5)
    return jnp.where(same_doc[None], scores, MASKED_SCORE)

def attend(queries, keys_all, values_all, same_doc):
    scores = masked_scores(queries, keys_all, same_doc)
    top_score = lax.optimization_barrier(jnp.max(scores, -1, keepdims=True))
    denominator = lax.optimization_barrier(jnp.sum(jnp.exp(scores - top_score), -1, keepdims=True))
    log_total = top_score + jnp.log(denominator)
    probs_low = jnp.exp(scores - log_total).astype(jnp.bfloat16)
    context = jnp.einsum('hqk,khe->qhe', probs_low.astype(jnp.float32), values_all.astype(jnp.float32))
    return (context, log_total)

def attend_back(queries, keys_all, values_all, same_doc, log_total, grad_context_low, context):
    scores = masked_scores(queries, keys_all, same_doc)
    probs = jnp.exp(scores - log_total)
    probs_low = probs.astype(jnp.bfloat16)
    grad_wide = grad_context_low.astype(jnp.float32)
    grad_probs = jnp.einsum('qhe,khe->hqk', grad_wide, values_all.astype(jnp.float32))
    delta_sum = lax.optimization_barrier(jnp.sum(grad_wide * context, -1))
    grad_scores = (probs * (grad_probs - jnp.transpose(delta_sum)[:, :, None]) * HEAD_DIM ** (-0.5)).astype(jnp.bfloat16)
    grad_queries = jnp.einsum('hqk,khe->qhe', grad_scores.astype(jnp.float32), keys_all.astype(jnp.float32))
    grad_keys = jnp.einsum('hqk,qhe->khe', grad_scores.astype(jnp.float32), queries.astype(jnp.float32))
    grad_values = jnp.einsum('hqk,qhe->khe', probs_low.astype(jnp.float32), grad_wide)
    return (grad_queries, grad_keys, grad_values)

def reference(tokens, segments, cotangent, w_query, w_key, w_value, w_output, w_inner, w_outer, b_query, b_value, b_output, gain_one, shift_one, b_inner, b_outer, gain_two, shift_two):
    parameters = (w_query, w_key, w_value, w_output, w_inner, w_outer, b_query, b_value, b_output, gain_one, shift_one, b_inner, b_outer, gain_two, shift_two)
    initial = tuple((jnp.zeros(parameter.shape, jnp.float32) for parameter in parameters))

    def one_sequence(totals, sequence_items):
        inputs, doc_ids, grad_result = sequence_items
        seq_rows = inputs.shape[0]
        model_width = inputs.shape[1]
        same_doc = doc_ids[:, None] == doc_ids[None, :]
        queries = (product(inputs, w_query) + b_query.astype(jnp.float32)).astype(jnp.bfloat16)
        keys_all = product(inputs, w_key).astype(jnp.bfloat16)
        values_all = (product(inputs, w_value) + b_value.astype(jnp.float32)).astype(jnp.bfloat16)
        head_q = queries.reshape(seq_rows, HEADS, HEAD_DIM)
        head_k = keys_all.reshape(seq_rows, HEADS, HEAD_DIM)
        head_v = values_all.reshape(seq_rows, HEADS, HEAD_DIM)
        context, log_total = attend(head_q, head_k, head_v, same_doc)
        context_low = context.reshape(seq_rows, model_width).astype(jnp.bfloat16)
        first_sum = inputs.astype(jnp.float32) + product(context_low, w_output) + b_output.astype(jnp.float32)
        first_out, first_normed, first_rstd = layer_norm(first_sum, gain_one, shift_one)
        first_low = first_out.astype(jnp.bfloat16)
        inner_pre = product(first_low, w_inner) + b_inner.astype(jnp.float32)
        normal_cdf, normal_pdf = normal_parts(inner_pre)
        activated = (inner_pre * normal_cdf).astype(jnp.bfloat16)
        second_sum = first_out + product(activated, w_outer) + b_outer.astype(jnp.float32)
        result, second_normed, second_rstd = layer_norm(second_sum, gain_two, shift_two)
        grad_gain_two = lax.optimization_barrier(jnp.sum(grad_result * second_normed, 0))
        grad_shift_two = lax.optimization_barrier(jnp.sum(grad_result, 0))
        grad_second = norm_back(grad_result, second_normed, second_rstd, gain_two)
        grad_second_low = grad_second.astype(jnp.bfloat16)
        grad_outer_bias = lax.optimization_barrier(jnp.sum(grad_second, 0))
        grad_act = times_transposed(grad_second_low, w_outer)
        grad_inner = grad_act * (normal_cdf + inner_pre * normal_pdf)
        grad_inner_low = grad_inner.astype(jnp.bfloat16)
        grad_inner_bias = lax.optimization_barrier(jnp.sum(grad_inner, 0))
        grad_first_out = grad_second + times_transposed(grad_inner_low, w_inner)
        grad_gain_one = lax.optimization_barrier(jnp.sum(grad_first_out * first_normed, 0))
        grad_shift_one = lax.optimization_barrier(jnp.sum(grad_first_out, 0))
        grad_first = norm_back(grad_first_out, first_normed, first_rstd, gain_one)
        grad_first_low = grad_first.astype(jnp.bfloat16)
        grad_output_bias = lax.optimization_barrier(jnp.sum(grad_first, 0))
        grad_context_low = times_transposed(grad_first_low, w_output).astype(jnp.bfloat16).reshape(seq_rows, HEADS, HEAD_DIM)
        grad_queries, grad_keys, grad_values = attend_back(head_q, head_k, head_v, same_doc, log_total, grad_context_low, context)
        grad_queries = grad_queries.reshape(seq_rows, model_width)
        grad_keys = grad_keys.reshape(seq_rows, model_width)
        grad_values = grad_values.reshape(seq_rows, model_width)
        grad_query_low = grad_queries.astype(jnp.bfloat16)
        grad_key_low = grad_keys.astype(jnp.bfloat16)
        grad_value_low = grad_values.astype(jnp.bfloat16)
        input_grad = grad_first + times_transposed(grad_query_low, w_query) + times_transposed(grad_key_low, w_key) + times_transposed(grad_value_low, w_value)
        terms = (transposed_times(inputs, grad_query_low), transposed_times(inputs, grad_key_low), transposed_times(inputs, grad_value_low), transposed_times(context_low, grad_first_low), transposed_times(first_low, grad_inner_low), transposed_times(activated, grad_second_low), lax.optimization_barrier(jnp.sum(grad_queries, 0)), lax.optimization_barrier(jnp.sum(grad_values, 0)), grad_output_bias, grad_gain_one, grad_shift_one, grad_inner_bias, grad_outer_bias, grad_gain_two, grad_shift_two)
        new_totals = tuple((total + term for total, term in zip(totals, terms)))
        return (new_totals, (result, input_grad))
    totals, outputs = lax.scan(one_sequence, initial, (tokens, segments, cotangent))
    return (outputs[0], outputs[1], totals[0], totals[1], totals[2], totals[3], totals[4], totals[5], totals[6], totals[7], totals[8], totals[9], totals[10], totals[11], totals[12], totals[13], totals[14])
```

```python
import functools

import jax
import jax.numpy as jnp
from jax import lax
from jax.experimental import pallas as pl
from jax.experimental.pallas import tpu as pltpu
from jax.sharding import PartitionSpec as P

HEAD_DIM = 64
EPSILON = 1e-12
MASKED_SCORE = -1e30
LANES = 128
HEAD_PAIR = LANES // HEAD_DIM
SCALE = HEAD_DIM**-0.5
KEY_STEP = 256

WIDE = jnp.float32
LOW = jnp.bfloat16


def product(left_side, right_side):
    return jnp.dot(left_side, right_side, preferred_element_type=WIDE)


def times_transposed(left_side, right_side):
    return lax.dot_general(
        left_side, right_side, (((1,), (1,)), ((), ())), preferred_element_type=WIDE
    )


def transposed_times(left_side, right_side):
    return lax.dot_general(
        left_side, right_side, (((0,), (0,)), ((), ())), preferred_element_type=WIDE
    )


def layer_norm(summed, gain_vec, shift_vec):
    row_mean = jnp.mean(summed, -1, keepdims=True)
    centred = summed - row_mean
    variance = jnp.mean(centred * centred, -1, keepdims=True)
    inv_std = lax.rsqrt(variance + EPSILON)
    normed = centred * inv_std
    return (normed * gain_vec + shift_vec, normed, inv_std)


def norm_back(upstream, normed, inv_std, gain_vec):
    scaled_grad = upstream * gain_vec
    first_term = jnp.mean(scaled_grad, -1, keepdims=True)
    second_term = jnp.mean(scaled_grad * normed, -1, keepdims=True)
    return inv_std * (scaled_grad - first_term - normed * second_term)


def normal_parts(inner_pre):
    normal_cdf = 0.5 * (1.0 + lax.erf(inner_pre * 0.7071067811865476))
    normal_pdf = jnp.exp(-0.5 * inner_pre * inner_pre) * 0.3989422804014327
    return (normal_cdf, normal_pdf)


def key_ranges(own_ids, doc_ids, block):
    total = doc_ids.shape[-1]
    blocks = own_ids.reshape(own_ids.shape[0], -1, block)
    first = blocks[:, :, 0]
    last = blocks[:, :, -1]
    begin = jnp.sum(doc_ids[:, None, :] < first[:, :, None], -1, dtype=jnp.int32)
    end = jnp.sum(doc_ids[:, None, :] <= last[:, :, None], -1, dtype=jnp.int32)
    start = begin // LANES
    steps = (end - start * LANES + KEY_STEP - 1) // KEY_STEP
    start = jnp.minimum(start, (total - steps * KEY_STEP) // LANES)
    return jnp.stack([start, steps - 1], -1).reshape(-1)


def head_lanes(rows, head):
    lane = lax.broadcasted_iota(jnp.int32, (rows, LANES), 1)
    return (lane >= head * HEAD_DIM) & (lane < (head + 1) * HEAD_DIM)


def only_head(array, head):
    return jnp.where(head_lanes(array.shape[0], head), array, jnp.zeros_like(array))


def by_width(steps, most, branch):
    lax.switch(steps, [functools.partial(branch, (n + 1) * KEY_STEP) for n in range(most)])


def masked(scores_t, key_ids, query_ids):
    wide_ids = jnp.tile(key_ids, (1, scores_t.shape[1] // LANES))
    return jnp.where(wide_ids == query_ids, scores_t, MASKED_SCORE)


def attend_kernel(block, ranges, q_ref, k_ref, v_ref, qid_ref, kid_ref, ctx_ref, low_ref, lse_ref):
    count = q_ref.shape[1] // block
    total = k_ref.shape[1]
    base = pl.program_id(0) * count

    def one_block(index, carry):
        rows = pl.ds(pl.multiple_of(index * block, block), block)
        start = pl.multiple_of(ranges[2 * (base + index)] * LANES, LANES)
        steps = ranges[2 * (base + index) + 1]

        def branch(width):
            keys = pl.ds(start, width)
            key_part = k_ref[0, keys, :]
            value_part = v_ref[0, keys, :]
            key_ids = kid_ref[0, keys, :]
            query_ids = qid_ref[0, :, rows]
            query_part = q_ref[0, rows, :] * jnp.asarray(SCALE, LOW)
            parts = []
            for head in range(HEAD_PAIR):
                scores = times_transposed(key_part, only_head(query_part, head))
                scores = masked(scores, key_ids, query_ids)
                top = jnp.max(scores, 0, keepdims=True)
                powers = jnp.exp(scores - top)
                denominator = jnp.sum(powers, 0, keepdims=True)
                probs_low = (powers * (1.0 / denominator)).astype(LOW)
                lse_ref[0, 0, head : head + 1, rows] = top + jnp.log(denominator)
                both = transposed_times(value_part, probs_low)
                parts.append(both[head * HEAD_DIM : (head + 1) * HEAD_DIM])
            context = jnp.transpose(jnp.concatenate(parts, 0))
            ctx_ref[0, rows, :] = context
            low_ref[0, rows, :] = context.astype(LOW)

        by_width(steps, total // KEY_STEP, branch)
        return carry

    lax.fori_loop(0, count, one_block, 0)


def attend_back_kernel(
    block,
    ranges,
    q_ref,
    k_ref,
    v_ref,
    g_ref,
    ctx_ref,
    lse_ref,
    qid_ref,
    kid_ref,
    dq_ref,
    dk_ref,
    dv_ref,
    dk_sum,
    dv_sum,
):
    count = q_ref.shape[1] // block
    total = k_ref.shape[1]
    base = pl.program_id(0) * count
    dk_sum[...] = jnp.zeros_like(dk_sum)
    dv_sum[...] = jnp.zeros_like(dv_sum)

    def one_block(index, carry):
        rows = pl.ds(pl.multiple_of(index * block, block), block)
        start = pl.multiple_of(ranges[2 * (base + index)] * LANES, LANES)
        steps = ranges[2 * (base + index) + 1]

        def branch(width):
            keys = pl.ds(start, width)
            key_part = k_ref[0, keys, :]
            value_part = v_ref[0, keys, :] * jnp.asarray(SCALE, LOW)
            key_ids = kid_ref[0, keys, :]
            query_ids = qid_ref[0, :, rows]
            query_part = q_ref[0, rows, :]
            grad_part = g_ref[0, rows, :]
            products = jnp.transpose(grad_part.astype(WIDE) * ctx_ref[0, rows, :])
            dq_parts = []
            dk_total = None
            dv_total = None
            for head in range(HEAD_PAIR):
                query_head = only_head(query_part, head)
                grad_head = only_head(grad_part, head)
                scores = times_transposed(key_part, query_head * jnp.asarray(SCALE, LOW))
                scores = masked(scores, key_ids, query_ids)
                probs = jnp.exp(scores - lse_ref[0, 0, head : head + 1, rows])
                probs_low = probs.astype(LOW)
                delta = SCALE * jnp.sum(
                    products[head * HEAD_DIM : (head + 1) * HEAD_DIM], 0, keepdims=True
                )
                grad_probs = times_transposed(value_part, grad_head)
                grad_scores = (probs * (grad_probs - delta)).astype(LOW)
                dv_part = product(probs_low, grad_head)
                dk_part = product(grad_scores, query_head)
                dq_parts.append(transposed_times(grad_scores, key_part))
                dk_total = dk_part if dk_total is None else dk_total + dk_part
                dv_total = dv_part if dv_total is None else dv_total + dv_part
            dq = dq_parts[0]
            for head in range(1, HEAD_PAIR):
                dq = jnp.where(head_lanes(block, head), dq_parts[head], dq)
            dq_ref[0, rows, :] = dq.astype(LOW)
            dk_sum[keys, :] += dk_total
            dv_sum[keys, :] += dv_total

        by_width(steps, total // KEY_STEP, branch)
        return carry

    lax.fori_loop(0, count, one_block, 0)
    dk_ref[0] = dk_sum[...].astype(LOW)
    dv_ref[0] = dv_sum[...].astype(LOW)


def attention_specs(queries, keys_all, block):
    seqs, length, width = queries.shape
    total = keys_all.shape[1]
    pairs = width // LANES
    per_query = pl.BlockSpec((1, length, LANES), lambda s, h, _: (s, 0, h))
    per_key = pl.BlockSpec((1, total, LANES), lambda s, h, _: (s, 0, h))
    lse_spec = pl.BlockSpec((1, 1, HEAD_PAIR, length), lambda s, h, _: (s, h, 0, 0))
    qid_spec = pl.BlockSpec((1, 1, length), lambda s, h, _: (s, 0, 0))
    kid_spec = pl.BlockSpec((1, total, LANES), lambda s, h, _: (s, 0, 0))
    return (seqs, pairs), per_query, per_key, lse_spec, qid_spec, kid_spec


def attend(queries, keys_all, values_all, tables):
    ranges, query_ids, key_ids, block = tables
    grid, per_query, per_key, lse_spec, qid_spec, kid_spec = attention_specs(
        queries, keys_all, block
    )
    seqs, length, width = queries.shape
    return pl.pallas_call(
        functools.partial(attend_kernel, block),
        grid_spec=pltpu.PrefetchScalarGridSpec(
            num_scalar_prefetch=1,
            grid=grid,
            in_specs=[per_query, per_key, per_key, qid_spec, kid_spec],
            out_specs=[per_query, per_query, lse_spec],
        ),
        out_shape=[
            jax.ShapeDtypeStruct(queries.shape, WIDE),
            jax.ShapeDtypeStruct(queries.shape, LOW),
            jax.ShapeDtypeStruct((seqs, grid[1], HEAD_PAIR, length), WIDE),
        ],
        name="attend",
    )(ranges, queries, keys_all, values_all, query_ids, key_ids)


def attend_back(queries, keys_all, values_all, grad_context, context, lse, tables):
    ranges, query_ids, key_ids, block = tables
    grid, per_query, per_key, lse_spec, qid_spec, kid_spec = attention_specs(
        queries, keys_all, block
    )
    total = keys_all.shape[1]
    return pl.pallas_call(
        functools.partial(attend_back_kernel, block),
        grid_spec=pltpu.PrefetchScalarGridSpec(
            num_scalar_prefetch=1,
            grid=grid,
            in_specs=[
                per_query,
                per_key,
                per_key,
                per_query,
                per_query,
                lse_spec,
                qid_spec,
                kid_spec,
            ],
            out_specs=[per_query, per_key, per_key],
            scratch_shapes=[pltpu.VMEM((total, LANES), WIDE), pltpu.VMEM((total, LANES), WIDE)],
        ),
        out_shape=[
            jax.ShapeDtypeStruct(queries.shape, LOW),
            jax.ShapeDtypeStruct(keys_all.shape, LOW),
            jax.ShapeDtypeStruct(keys_all.shape, LOW),
        ],
        name="attend_back",
    )(ranges, queries, keys_all, values_all, grad_context, context, lse, query_ids, key_ids)


def swap_in(array, ranks, rank):
    part = array.shape[1]
    whole = jnp.zeros((1, ranks * part) + array.shape[2:], array.dtype)
    for shift in range(ranks):
        other = (rank + shift) % ranks
        piece = lax.dynamic_slice_in_dim(array, other, 1, 0)
        if shift:
            piece = lax.ppermute(piece, "ctx", [(i, (i + shift) % ranks) for i in range(ranks)])
        source = (rank + ranks - shift) % ranks
        whole = lax.dynamic_update_slice_in_dim(whole, piece, source * part, 1)
    return whole


def swap_out(array, ranks, rank):
    part = array.shape[1] // ranks
    spread = jnp.zeros((ranks, part) + array.shape[2:], array.dtype)
    for shift in range(ranks):
        other = (rank + shift) % ranks
        piece = lax.dynamic_slice_in_dim(array, other * part, part, 1)
        if shift:
            piece = lax.ppermute(piece, "ctx", [(i, (i + shift) % ranks) for i in range(ranks)])
        source = (rank + ranks - shift) % ranks
        spread = lax.dynamic_update_slice_in_dim(spread, piece, source, 0)
    return spread


def pack_blocks(matrices, vectors, width, lead):
    blocks = []
    for matrix in matrices:
        rows, columns = matrix.shape[-2:]
        if columns == width:
            blocks.append(matrix)
        else:
            for at in range(columns // width):
                blocks.append(matrix[..., at * width : (at + 1) * width])
    line = jnp.concatenate(vectors, -1)
    size = line.shape[-1]
    lines = -(-size // width)
    lines = -(-lines // 8) * 8
    pad = [(0, 0)] * lead + [(0, lines * width - size)]
    blocks.append(jnp.pad(line, pad).reshape(line.shape[:-1] + (lines, width)))
    return jnp.concatenate(blocks, -2)


def unpack_blocks(packed, matrices, vectors, width):
    out = []
    at = 0
    for matrix in matrices:
        rows, columns = matrix.shape
        pieces = []
        for _ in range(columns // width):
            pieces.append(packed[..., at : at + rows, :])
            at += rows
        out.append(pieces[0] if len(pieces) == 1 else jnp.concatenate(pieces, -1))
    line = packed[..., at:, :].reshape(packed.shape[:-2] + (-1,))
    at = 0
    for vector in vectors:
        size = vector.shape[0]
        out.append(line[..., at : at + size])
        at += size
    return out


def body(tokens, segments, cotangent, *shards):
    matrices, vectors = shards[:6], shards[6:]
    owners = lax.axis_size(("dp", "ctx"))
    ranks = lax.axis_size("ctx")
    rank = lax.axis_index("ctx")
    micro_count, local_len, width = tokens.shape
    whole_here = micro_count == ranks

    with jax.named_scope("gather"):
        packed = pack_blocks(matrices, vectors, width, 0)
        gathered = lax.all_gather(packed, ("dp", "ctx"), axis=0, tiled=False)
        wholes = unpack_blocks(gathered, matrices, vectors, width)
        query_mat, key_mat, value_mat, output_mat, inner_mat, outer_mat = [
            whole.reshape((-1,) + whole.shape[2:]) for whole in wholes[:6]
        ]
        (
            query_bias,
            value_bias,
            output_bias,
            gain_first,
            shift_first,
            inner_bias,
            outer_bias,
            gain_second,
            shift_second,
        ) = [whole.reshape(-1).astype(WIDE) for whole in wholes[6:]]

    with jax.named_scope("swap_in"):
        if whole_here:
            inputs = swap_in(tokens, ranks, rank)
            grad_result = swap_in(cotangent, ranks, rank)
            doc_ids = lax.dynamic_slice_in_dim(segments, rank, 1, 0)
            own_ids = doc_ids
        else:
            inputs, grad_result, doc_ids = tokens, cotangent, segments
            own_ids = lax.dynamic_slice_in_dim(doc_ids, rank * local_len, local_len, 1)
    seqs, length, _ = inputs.shape
    total = doc_ids.shape[1]
    block = min(256, length)
    tables = (
        key_ranges(own_ids, doc_ids, block),
        own_ids[:, None, :],
        jnp.broadcast_to(doc_ids[:, :, None], doc_ids.shape + (LANES,)),
        block,
    )
    by_seq = lambda array: array.reshape(seqs, -1, width)
    inputs = inputs.reshape(-1, width)
    grad_result = grad_result.reshape(-1, width)

    def all_keys(own):
        own = by_seq(own)
        return own if whole_here else lax.all_gather(own, "ctx", axis=1, tiled=True)

    def own_keys(terms):
        if not whole_here:
            terms = lax.psum_scatter(terms, "ctx", scatter_dimension=1, tiled=True)
        return terms.reshape(-1, width)

    with jax.named_scope("forward"):
        queries = by_seq((product(inputs, query_mat) + query_bias).astype(LOW))
        keys_all = all_keys(product(inputs, key_mat).astype(LOW))
        values_all = all_keys((product(inputs, value_mat) + value_bias).astype(LOW))
        context, context_low, lse = attend(queries, keys_all, values_all, tables)
        context_low = context_low.reshape(-1, width)
        first_sum = inputs.astype(WIDE) + product(context_low, output_mat) + output_bias
        first_out, first_normed, first_rstd = layer_norm(first_sum, gain_first, shift_first)
        first_low = first_out.astype(LOW)
        inner_pre = product(first_low, inner_mat) + inner_bias
        normal_cdf, normal_pdf = normal_parts(inner_pre)
        activated = (inner_pre * normal_cdf).astype(LOW)
        second_sum = first_out + product(activated, outer_mat) + outer_bias
        result, second_normed, second_rstd = layer_norm(second_sum, gain_second, shift_second)

    with jax.named_scope("backward"):
        grad_gain_two = jnp.sum(grad_result * second_normed, 0)
        grad_shift_two = jnp.sum(grad_result, 0)
        grad_second = norm_back(grad_result, second_normed, second_rstd, gain_second)
        grad_second_low = grad_second.astype(LOW)
        grad_outer_bias = jnp.sum(grad_second, 0)
        grad_act = times_transposed(grad_second_low, outer_mat)
        grad_inner = grad_act * (normal_cdf + inner_pre * normal_pdf)
        grad_inner_low = grad_inner.astype(LOW)
        grad_inner_bias = jnp.sum(grad_inner, 0)
        grad_first_out = grad_second + times_transposed(grad_inner_low, inner_mat)
        grad_gain_one = jnp.sum(grad_first_out * first_normed, 0)
        grad_shift_one = jnp.sum(grad_first_out, 0)
        grad_first = norm_back(grad_first_out, first_normed, first_rstd, gain_first)
        grad_first_low = grad_first.astype(LOW)
        grad_output_bias = jnp.sum(grad_first, 0)
        grad_context = by_seq(times_transposed(grad_first_low, output_mat).astype(LOW))
        dq, dk, dv = attend_back(
            queries, keys_all, values_all, grad_context, context, lse, tables
        )
        grad_query_low = dq.reshape(-1, width)
        grad_key_low = own_keys(dk)
        grad_value_low = own_keys(dv)
        input_grad = (
            grad_first
            + times_transposed(grad_query_low, query_mat)
            + times_transposed(grad_key_low, key_mat)
            + times_transposed(grad_value_low, value_mat)
        )
        matrix_terms = (
            transposed_times(inputs, grad_query_low),
            transposed_times(inputs, grad_key_low),
            transposed_times(inputs, grad_value_low),
            transposed_times(context_low, grad_first_low),
            transposed_times(first_low, grad_inner_low),
            transposed_times(activated, grad_second_low),
        )
        vector_terms = (
            jnp.sum(grad_query_low.astype(WIDE), 0),
            jnp.sum(grad_value_low.astype(WIDE), 0),
            grad_output_bias,
            grad_gain_one,
            grad_shift_one,
            grad_inner_bias,
            grad_outer_bias,
            grad_gain_two,
            grad_shift_two,
        )

    with jax.named_scope("scatter"):
        packed_terms = pack_blocks(
            [term.astype(LOW).reshape(owners, -1, term.shape[1]) for term in matrix_terms],
            [term.astype(LOW).reshape(owners, -1) for term in vector_terms],
            width,
            1,
        )
        owned = lax.psum_scatter(
            packed_terms, ("dp", "ctx"), scatter_dimension=0, tiled=False
        ).astype(WIDE)
        owned_grads = unpack_blocks(owned, matrices, vectors, width)

    with jax.named_scope("swap_out"):
        if whole_here:
            results = swap_out(by_seq(result), ranks, rank)
            input_grads = swap_out(by_seq(input_grad).astype(LOW), ranks, rank).astype(WIDE)
        else:
            results, input_grads = by_seq(result), by_seq(input_grad)
    return (results, input_grads) + tuple(owned_grads)


def solution(mesh):
    by_tokens = P("dp", "ctx", None)
    matrix = P(("dp", "ctx"), None)
    vector = P(("dp", "ctx"))
    grads = (matrix,) * 6 + (vector,) * 9
    in_specs = (by_tokens, P("dp", None), by_tokens) + grads
    out_specs = (by_tokens, by_tokens) + grads
    return jax.shard_map(body, mesh=mesh, in_specs=in_specs, out_specs=out_specs, check_vma=False)
```

```python
import functools

import jax
import jax.numpy as jnp
from jax import lax
from jax.experimental import pallas as pl
from jax.experimental.pallas import tpu as pltpu
from jax.sharding import PartitionSpec as P

HEAD_DIM = 64
EPSILON = 1e-12
MASKED_SCORE = -1e30
LANES = 128
HEAD_PAIR = LANES // HEAD_DIM
SCALE = HEAD_DIM**-0.5
KEY_STEP = 256

WIDE = jnp.float32
LOW = jnp.bfloat16


def product(left_side, right_side):
    return jnp.dot(left_side, right_side, preferred_element_type=WIDE)


def times_transposed(left_side, right_side):
    return lax.dot_general(
        left_side, right_side, (((1,), (1,)), ((), ())), preferred_element_type=WIDE
    )


def transposed_times(left_side, right_side):
    return lax.dot_general(
        left_side, right_side, (((0,), (0,)), ((), ())), preferred_element_type=WIDE
    )


def layer_norm(summed, gain_vec, shift_vec):
    row_mean = jnp.mean(summed, -1, keepdims=True)
    centred = summed - row_mean
    variance = jnp.mean(centred * centred, -1, keepdims=True)
    inv_std = lax.rsqrt(variance + EPSILON)
    normed = centred * inv_std
    return (normed * gain_vec + shift_vec, normed, inv_std)


def norm_back(upstream, normed, inv_std, gain_vec):
    scaled_grad = upstream * gain_vec
    first_term = jnp.mean(scaled_grad, -1, keepdims=True)
    second_term = jnp.mean(scaled_grad * normed, -1, keepdims=True)
    return inv_std * (scaled_grad - first_term - normed * second_term)


def normal_parts(inner_pre):
    normal_cdf = 0.5 * (1.0 + lax.erf(inner_pre * 0.7071067811865476))
    normal_pdf = jnp.exp(-0.5 * inner_pre * inner_pre) * 0.3989422804014327
    return (normal_cdf, normal_pdf)


def key_ranges(own_ids, doc_ids, block):
    total = doc_ids.shape[-1]
    blocks = own_ids.reshape(own_ids.shape[0], -1, block)
    first = blocks[:, :, 0]
    last = blocks[:, :, -1]
    begin = jnp.sum(doc_ids[:, None, :] < first[:, :, None], -1, dtype=jnp.int32)
    end = jnp.sum(doc_ids[:, None, :] <= last[:, :, None], -1, dtype=jnp.int32)
    start = begin // LANES
    steps = (end - start * LANES + KEY_STEP - 1) // KEY_STEP
    start = jnp.minimum(start, (total - steps * KEY_STEP) // LANES)
    return jnp.stack([start, steps - 1], -1).reshape(-1)


def head_lanes(rows, head):
    lane = lax.broadcasted_iota(jnp.int32, (rows, LANES), 1)
    return (lane >= head * HEAD_DIM) & (lane < (head + 1) * HEAD_DIM)


def only_head(array, head):
    return jnp.where(head_lanes(array.shape[0], head), array, jnp.zeros_like(array))


def folded(array, combine):
    while array.shape[0] % 16 == 0:
        half = array.shape[0] // 2
        array = combine(array[:half], array[half:])
    return array


def by_width(steps, most, branch):
    lax.switch(steps, [functools.partial(branch, (n + 1) * KEY_STEP) for n in range(most)])


def masked(scores_t, key_ids, query_ids):
    wide_ids = jnp.tile(key_ids, (1, scores_t.shape[1] // LANES))
    return jnp.where(wide_ids == query_ids, scores_t, MASKED_SCORE)


def attend_kernel(block, ranges, q_ref, k_ref, v_ref, qid_ref, kid_ref, ctx_ref, low_ref, lse_ref):
    count = q_ref.shape[1] // block
    total = k_ref.shape[1]
    base = pl.program_id(0) * count

    def one_block(index, carry):
        rows = pl.ds(pl.multiple_of(index * block, block), block)
        start = pl.multiple_of(ranges[2 * (base + index)] * LANES, LANES)
        steps = ranges[2 * (base + index) + 1]

        def branch(width):
            keys = pl.ds(start, width)
            key_part = k_ref[0, keys, :]
            value_part = v_ref[0, keys, :]
            key_ids = kid_ref[0, keys, :]
            query_ids = qid_ref[0, :, rows]
            query_part = q_ref[0, rows, :] * jnp.asarray(SCALE, LOW)
            parts = []
            for head in range(HEAD_PAIR):
                scores = times_transposed(key_part, only_head(query_part, head))
                scores = masked(scores, key_ids, query_ids)
                top = jnp.max(folded(scores, jnp.maximum), 0, keepdims=True)
                powers = jnp.exp(scores - top)
                denominator = jnp.sum(folded(powers, jnp.add), 0, keepdims=True)
                probs_low = (powers * (1.0 / denominator)).astype(LOW)
                lse_ref[0, 0, head : head + 1, rows] = top + jnp.log(denominator)
                both = transposed_times(value_part, probs_low)
                parts.append(both[head * HEAD_DIM : (head + 1) * HEAD_DIM])
            context = jnp.transpose(jnp.concatenate(parts, 0))
            ctx_ref[0, rows, :] = context
            low_ref[0, rows, :] = context.astype(LOW)

        by_width(steps, total // KEY_STEP, branch)
        return carry

    lax.fori_loop(0, count, one_block, 0)


def attend_back_kernel(
    block,
    ranges,
    q_ref,
    k_ref,
    v_ref,
    g_ref,
    ctx_ref,
    lse_ref,
    qid_ref,
    kid_ref,
    dq_ref,
    dk_ref,
    dv_ref,
    dk_sum,
    dv_sum,
):
    count = q_ref.shape[1] // block
    total = k_ref.shape[1]
    base = pl.program_id(0) * count
    dk_sum[...] = jnp.zeros_like(dk_sum)
    dv_sum[...] = jnp.zeros_like(dv_sum)

    def one_block(index, carry):
        rows = pl.ds(pl.multiple_of(index * block, block), block)
        start = pl.multiple_of(ranges[2 * (base + index)] * LANES, LANES)
        steps = ranges[2 * (base + index) + 1]

        def branch(width):
            keys = pl.ds(start, width)
            key_part = k_ref[0, keys, :]
            value_part = v_ref[0, keys, :] * jnp.asarray(SCALE, LOW)
            key_ids = kid_ref[0, keys, :]
            query_ids = qid_ref[0, :, rows]
            query_part = q_ref[0, rows, :]
            grad_part = g_ref[0, rows, :]
            products = jnp.transpose(grad_part.astype(WIDE) * ctx_ref[0, rows, :])
            dq_parts = []
            dk_total = None
            dv_total = None
            for head in range(HEAD_PAIR):
                query_head = only_head(query_part, head)
                grad_head = only_head(grad_part, head)
                scores = times_transposed(key_part, query_head * jnp.asarray(SCALE, LOW))
                scores = masked(scores, key_ids, query_ids)
                probs = jnp.exp(scores - lse_ref[0, 0, head : head + 1, rows])
                probs_low = probs.astype(LOW)
                delta = SCALE * jnp.sum(
                    products[head * HEAD_DIM : (head + 1) * HEAD_DIM], 0, keepdims=True
                )
                grad_probs = times_transposed(value_part, grad_head)
                grad_scores = (probs * (grad_probs - delta)).astype(LOW)
                dv_part = product(probs_low, grad_head)
                dk_part = product(grad_scores, query_head)
                dq_parts.append(transposed_times(grad_scores, key_part))
                dk_total = dk_part if dk_total is None else dk_total + dk_part
                dv_total = dv_part if dv_total is None else dv_total + dv_part
            dq = dq_parts[0]
            for head in range(1, HEAD_PAIR):
                dq = jnp.where(head_lanes(block, head), dq_parts[head], dq)
            dq_ref[0, rows, :] = dq.astype(LOW)
            dk_sum[keys, :] += dk_total
            dv_sum[keys, :] += dv_total

        by_width(steps, total // KEY_STEP, branch)
        return carry

    lax.fori_loop(0, count, one_block, 0)
    dk_ref[0] = dk_sum[...].astype(LOW)
    dv_ref[0] = dv_sum[...].astype(LOW)


def attention_specs(queries, keys_all, block):
    seqs, length, width = queries.shape
    total = keys_all.shape[1]
    pairs = width // LANES
    per_query = pl.BlockSpec((1, length, LANES), lambda s, h, _: (s, 0, h))
    per_key = pl.BlockSpec((1, total, LANES), lambda s, h, _: (s, 0, h))
    lse_spec = pl.BlockSpec((1, 1, HEAD_PAIR, length), lambda s, h, _: (s, h, 0, 0))
    qid_spec = pl.BlockSpec((1, 1, length), lambda s, h, _: (s, 0, 0))
    kid_spec = pl.BlockSpec((1, total, LANES), lambda s, h, _: (s, 0, 0))
    return (seqs, pairs), per_query, per_key, lse_spec, qid_spec, kid_spec


def attend(queries, keys_all, values_all, tables):
    ranges, query_ids, key_ids, block = tables
    grid, per_query, per_key, lse_spec, qid_spec, kid_spec = attention_specs(
        queries, keys_all, block
    )
    seqs, length, width = queries.shape
    return pl.pallas_call(
        functools.partial(attend_kernel, block),
        grid_spec=pltpu.PrefetchScalarGridSpec(
            num_scalar_prefetch=1,
            grid=grid,
            in_specs=[per_query, per_key, per_key, qid_spec, kid_spec],
            out_specs=[per_query, per_query, lse_spec],
        ),
        out_shape=[
            jax.ShapeDtypeStruct(queries.shape, WIDE),
            jax.ShapeDtypeStruct(queries.shape, LOW),
            jax.ShapeDtypeStruct((seqs, grid[1], HEAD_PAIR, length), WIDE),
        ],
        name="attend",
    )(ranges, queries, keys_all, values_all, query_ids, key_ids)


def attend_back(queries, keys_all, values_all, grad_context, context, lse, tables):
    ranges, query_ids, key_ids, block = tables
    grid, per_query, per_key, lse_spec, qid_spec, kid_spec = attention_specs(
        queries, keys_all, block
    )
    total = keys_all.shape[1]
    return pl.pallas_call(
        functools.partial(attend_back_kernel, block),
        grid_spec=pltpu.PrefetchScalarGridSpec(
            num_scalar_prefetch=1,
            grid=grid,
            in_specs=[
                per_query,
                per_key,
                per_key,
                per_query,
                per_query,
                lse_spec,
                qid_spec,
                kid_spec,
            ],
            out_specs=[per_query, per_key, per_key],
            scratch_shapes=[pltpu.VMEM((total, LANES), WIDE), pltpu.VMEM((total, LANES), WIDE)],
        ),
        out_shape=[
            jax.ShapeDtypeStruct(queries.shape, LOW),
            jax.ShapeDtypeStruct(keys_all.shape, LOW),
            jax.ShapeDtypeStruct(keys_all.shape, LOW),
        ],
        name="attend_back",
    )(ranges, queries, keys_all, values_all, grad_context, context, lse, query_ids, key_ids)


def exchange(pieces, ranks):
    arrived = [pieces[0]]
    for shift in range(1, ranks):
        pairs = [(i, (i + shift) % ranks) for i in range(ranks)]
        arrived.append(lax.ppermute(pieces[shift], "ctx", pairs))
    return arrived


def in_order(arrived, rank, axis):
    ranks = len(arrived)
    return jnp.concatenate(
        [lax.select_n((rank + ranks - at) % ranks, *arrived) for at in range(ranks)]
        if ranks > 2
        else [jnp.where(rank == at, arrived[0], arrived[1]) for at in range(ranks)],
        axis,
    )


def swap_in(array, ranks, rank):
    pieces = [
        lax.dynamic_slice_in_dim(array, (rank + shift) % ranks, 1, 0) for shift in range(ranks)
    ]
    return in_order(exchange(pieces, ranks), rank, 1)


def swap_out(array, ranks, rank):
    part = array.shape[1] // ranks
    pieces = [
        lax.dynamic_slice_in_dim(array, (rank + shift) % ranks * part, part, 1)
        for shift in range(ranks)
    ]
    return in_order(exchange(pieces, ranks), rank, 0)


COLORS = 3


def owner_bits(dp_size, ctx_size):
    dp_bits = [("dp", at) for at in reversed(range(dp_size.bit_length() - 1))]
    return dp_bits + [("ctx", at) for at in reversed(range(ctx_size.bit_length() - 1))]


def halving_order(bits, color):
    near, far = ("dp", 0), bits[0]
    middle = [bit for bit in bits if bit not in (near, far)]
    middle.reverse()
    turn = color % max(len(middle), 1)
    return [near] + middle[turn:] + middle[:turn] + ([far] if far != near else [])


def own_bit(bit):
    axis, at = bit
    return (lax.axis_index(axis) >> at) & 1


def to_partner(array, bit):
    axis, at = bit
    return lax.ppermute(array, axis, [(i, i ^ (1 << at)) for i in range(lax.axis_size(axis))])


def scatter_sum(blocks, bits, color):
    first, *others = halving_order(bits, color)
    left = list(bits)
    shape = (2,) * len(bits)
    at = left.index(first)
    blocks = [block.reshape(shape + block.shape[1:]) for block in blocks]
    pick = lambda array, which, where: lax.dynamic_index_in_dim(array, which, where, keepdims=False)
    mine = [pick(block, own_bit(first), at) for block in blocks]
    away = jnp.concatenate([pick(block, 1 - own_bit(first), at).astype(LOW) for block in blocks], -2)
    came = to_partner(away, first)
    left.pop(at)
    rows = 0
    sums = []
    for part in mine:
        more = came[..., rows : rows + part.shape[-2], :]
        sums.append((part + more.astype(WIDE)).astype(LOW))
        rows += part.shape[-2]
    total = jnp.concatenate(sums, -2)
    for bit in others:
        at = left.index(bit)
        came = to_partner(pick(total, 1 - own_bit(bit), at), bit)
        total = pick(total, own_bit(bit), at).astype(WIDE) + came.astype(WIDE)
        total = total.astype(LOW) if bit != others[-1] else total
        left.pop(at)
    return total.astype(WIDE)


def gather_all(own, bits, color):
    have = []
    for bit in reversed(halving_order(bits, color)):
        came = to_partner(own, bit)
        at = sum(bits.index(other) < bits.index(bit) for other in have)
        low, high = jnp.where(own_bit(bit) == 0, own, came), jnp.where(own_bit(bit) == 0, came, own)
        own = jnp.stack([low, high], at)
        have.append(bit)
    return own.reshape((-1,) + own.shape[len(bits) :])


def column_blocks(matrix, width):
    return [
        matrix[..., at * width : (at + 1) * width] for at in range(matrix.shape[-1] // width)
    ]


def row_blocks(matrix, count):
    rows = matrix.shape[-2] // count
    return [matrix[..., at * rows : (at + 1) * rows, :] for at in range(count)]


def vector_block(vectors, width):
    line = jnp.concatenate(vectors, -1)
    size = line.shape[-1]
    lines = -(-(-(-size // width)) // 8) * 8
    line = jnp.pad(line, [(0, 0)] * (line.ndim - 1) + [(0, lines * width - size)])
    return line.reshape(line.shape[:-1] + (lines, width))


def from_vector_block(block, shards):
    line = block.reshape(block.shape[:-2] + (-1,))
    vectors, at = [], 0
    for shard in shards:
        vectors.append(line[..., at : at + shard.shape[0]])
        at += shard.shape[0]
    return vectors


def body(tokens, segments, cotangent, *shards):
    matrices, vectors = shards[:6], shards[6:]
    dp_size, ranks = lax.axis_size("dp"), lax.axis_size("ctx")
    owners = dp_size * ranks
    rank = lax.axis_index("ctx")
    micro_count, local_len, width = tokens.shape
    whole_here = micro_count == ranks
    bits = owner_bits(dp_size, ranks)
    own_rows = matrices[0].shape[0]
    joined = lambda whole: whole.reshape(-1, whole.shape[-1])

    with jax.named_scope("gather"):
        later = jnp.concatenate(
            [matrices[3]] + column_blocks(matrices[4], width) + [matrices[5]], 0
        )
        later = lax.all_gather(later, ("dp", "ctx"), axis=0, tiled=False)
        sent = [matrices[0], matrices[1], jnp.concatenate([matrices[2], vector_block(vectors, width)], 0)]
        query_mat, key_mat, last = [gather_all(own, bits, at) for at, own in enumerate(sent)]
        value_mat = joined(last[:, :own_rows])
        query_mat, key_mat = joined(query_mat), joined(key_mat)
        (
            query_bias,
            value_bias,
            output_bias,
            gain_first,
            shift_first,
            inner_bias,
            outer_bias,
            gain_second,
            shift_second,
        ) = [whole.reshape(-1).astype(WIDE) for whole in from_vector_block(last[:, own_rows:], vectors)]
        inner_count = matrices[4].shape[1] // width
        output_mat = joined(later[:, :own_rows])
        inner_mat = jnp.concatenate(
            [
                joined(later[:, (1 + at) * own_rows : (2 + at) * own_rows])
                for at in range(inner_count)
            ],
            1,
        )
        outer_mat = joined(later[:, (1 + inner_count) * own_rows :])

    with jax.named_scope("swap_in"):
        if whole_here:
            inputs = swap_in(tokens, ranks, rank)
            doc_ids = lax.dynamic_slice_in_dim(segments, rank, 1, 0)
            own_ids = doc_ids
        else:
            inputs, doc_ids = tokens, segments
            own_ids = lax.dynamic_slice_in_dim(doc_ids, rank * local_len, local_len, 1)
    seqs, length, _ = inputs.shape
    block = min(256, length)
    tables = (
        key_ranges(own_ids, doc_ids, block),
        own_ids[:, None, :],
        jnp.broadcast_to(doc_ids[:, :, None], doc_ids.shape + (LANES,)),
        block,
    )
    by_seq = lambda array: array.reshape(seqs, -1, width)
    inputs = inputs.reshape(-1, width)

    def all_keys(own):
        own = by_seq(own)
        return own if whole_here else lax.all_gather(own, "ctx", axis=1, tiled=True)

    def own_keys(terms):
        if not whole_here:
            terms = lax.psum_scatter(terms, "ctx", scatter_dimension=1, tiled=True)
        return terms.reshape(-1, width)

    with jax.named_scope("forward"):
        queries = by_seq((product(inputs, query_mat) + query_bias).astype(LOW))
        keys_all = all_keys(product(inputs, key_mat).astype(LOW))
        values_all = all_keys((product(inputs, value_mat) + value_bias).astype(LOW))
        context, context_low, lse = attend(queries, keys_all, values_all, tables)
        if whole_here:
            cotangent, _ = lax.optimization_barrier((cotangent, query_mat))
            grad_result = swap_in(cotangent, ranks, rank)
        else:
            grad_result = cotangent
        grad_result = grad_result.reshape(-1, width)
        context_low = context_low.reshape(-1, width)
        first_sum = inputs.astype(WIDE) + product(context_low, output_mat) + output_bias
        first_out, first_normed, first_rstd = layer_norm(first_sum, gain_first, shift_first)
        first_low = first_out.astype(LOW)
        inner_pre = product(first_low, inner_mat) + inner_bias
        normal_cdf, normal_pdf = normal_parts(inner_pre)
        activated = (inner_pre * normal_cdf).astype(LOW)
        second_sum = first_out + product(activated, outer_mat) + outer_bias
        result, second_normed, second_rstd = layer_norm(second_sum, gain_second, shift_second)

    with jax.named_scope("backward"):
        grad_gain_two = jnp.sum(grad_result * second_normed, 0)
        grad_shift_two = jnp.sum(grad_result, 0)
        grad_second = norm_back(grad_result, second_normed, second_rstd, gain_second)
        grad_second_low = grad_second.astype(LOW)
        grad_outer_bias = jnp.sum(grad_second, 0)
        grad_act = times_transposed(grad_second_low, outer_mat)
        grad_inner = grad_act * (normal_cdf + inner_pre * normal_pdf)
        grad_inner_low = grad_inner.astype(LOW)
        grad_inner_bias = jnp.sum(grad_inner, 0)
        grad_first_out = grad_second + times_transposed(grad_inner_low, inner_mat)
        grad_gain_one = jnp.sum(grad_first_out * first_normed, 0)
        grad_shift_one = jnp.sum(grad_first_out, 0)
        grad_first = norm_back(grad_first_out, first_normed, first_rstd, gain_first)
        grad_first_low = grad_first.astype(LOW)
        grad_output_bias = jnp.sum(grad_first, 0)
        by_owner = lambda term: term.reshape(owners, -1, term.shape[1])
        early = (
            [by_owner(transposed_times(context_low, grad_first_low))]
            + column_blocks(by_owner(transposed_times(first_low, grad_inner_low)), width)
            + row_blocks(by_owner(transposed_times(activated, grad_second_low)), inner_count)
        )
        cuts = [len(early) * at // COLORS for at in range(COLORS + 1)]
        early_sums = [
            scatter_sum(early[cuts[at] : cuts[at + 1]], bits, at) for at in range(COLORS)
        ]
        grad_context = by_seq(times_transposed(grad_first_low, output_mat).astype(LOW))
        dq, dk, dv = attend_back(
            queries, keys_all, values_all, grad_context, context, lse, tables
        )
        grad_query_low = dq.reshape(-1, width)
        grad_key_low = own_keys(dk)
        grad_value_low = own_keys(dv)
        late = [
            by_owner(transposed_times(inputs, grad_low))
            for grad_low in (grad_query_low, grad_key_low, grad_value_low)
        ]
        vector_terms = (
            jnp.sum(grad_query_low.astype(WIDE), 0),
            jnp.sum(grad_value_low.astype(WIDE), 0),
            grad_output_bias,
            grad_gain_one,
            grad_shift_one,
            grad_inner_bias,
            grad_outer_bias,
            grad_gain_two,
            grad_shift_two,
        )
        lines = vector_block([term.reshape(owners, -1) for term in vector_terms], width)
        late_sums = [
            scatter_sum([late[0]], bits, 0),
            scatter_sum([late[1]], bits, 1),
            scatter_sum([late[2], lines], bits, 2),
        ]
        input_grad = (
            grad_first
            + times_transposed(grad_query_low, query_mat)
            + times_transposed(grad_key_low, key_mat)
            + times_transposed(grad_value_low, value_mat)
        )

    with jax.named_scope("owned"):
        rows = row_blocks(jnp.concatenate(early_sums, 0), len(early))
        own_lines = late_sums[2][own_rows:]
        owned_grads = [
            late_sums[0],
            late_sums[1],
            late_sums[2][:own_rows],
            rows[0],
            jnp.concatenate(rows[1 : 1 + inner_count], 1),
            jnp.concatenate(rows[1 + inner_count :], 0),
        ] + from_vector_block(own_lines, vectors)

    with jax.named_scope("swap_out"):
        if whole_here:
            results = swap_out(by_seq(result), ranks, rank)
            input_grads = swap_out(by_seq(input_grad).astype(LOW), ranks, rank).astype(WIDE)
        else:
            results, input_grads = by_seq(result), by_seq(input_grad)
    return (results, input_grads) + tuple(owned_grads)


def solution(mesh):
    by_tokens = P("dp", "ctx", None)
    matrix = P(("dp", "ctx"), None)
    vector = P(("dp", "ctx"))
    grads = (matrix,) * 6 + (vector,) * 9
    in_specs = (by_tokens, P("dp", None), by_tokens) + grads
    out_specs = (by_tokens, by_tokens) + grads
    return jax.shard_map(body, mesh=mesh, in_specs=in_specs, out_specs=out_specs, check_vma=False)
```

```python
import functools

import jax
import jax.numpy as jnp
from jax import lax
from jax.experimental import pallas as pl
from jax.experimental.pallas import tpu as pltpu
from jax.sharding import PartitionSpec as P

HEAD_DIM = 64
EPSILON = 1e-12
MASKED_SCORE = -1e30
LANES = 128
HEAD_PAIR = LANES // HEAD_DIM
SCALE = HEAD_DIM**-0.5
KEY_STEP = 256

WIDE = jnp.float32
LOW = jnp.bfloat16


def product(left_side, right_side):
    return jnp.dot(left_side, right_side, preferred_element_type=WIDE)


def times_transposed(left_side, right_side):
    return lax.dot_general(
        left_side, right_side, (((1,), (1,)), ((), ())), preferred_element_type=WIDE
    )


def transposed_times(left_side, right_side):
    return lax.dot_general(
        left_side, right_side, (((0,), (0,)), ((), ())), preferred_element_type=WIDE
    )


def layer_norm(summed, gain_vec, shift_vec):
    row_mean = jnp.mean(summed, -1, keepdims=True)
    centred = summed - row_mean
    variance = jnp.mean(centred * centred, -1, keepdims=True)
    inv_std = lax.rsqrt(variance + EPSILON)
    normed = centred * inv_std
    return (normed * gain_vec + shift_vec, normed, inv_std)


def norm_back(upstream, normed, inv_std, gain_vec):
    scaled_grad = upstream * gain_vec
    first_term = jnp.mean(scaled_grad, -1, keepdims=True)
    second_term = jnp.mean(scaled_grad * normed, -1, keepdims=True)
    return inv_std * (scaled_grad - first_term - normed * second_term)


def normal_parts(inner_pre):
    normal_cdf = 0.5 * (1.0 + lax.erf(inner_pre * 0.7071067811865476))
    normal_pdf = jnp.exp(-0.5 * inner_pre * inner_pre) * 0.3989422804014327
    return (normal_cdf, normal_pdf)


def key_ranges(own_ids, doc_ids, block):
    total = doc_ids.shape[-1]
    blocks = own_ids.reshape(own_ids.shape[0], -1, block)
    first = blocks[:, :, 0]
    last = blocks[:, :, -1]
    begin = jnp.sum(doc_ids[:, None, :] < first[:, :, None], -1, dtype=jnp.int32)
    end = jnp.sum(doc_ids[:, None, :] <= last[:, :, None], -1, dtype=jnp.int32)
    start = begin // LANES
    steps = (end - start * LANES + KEY_STEP - 1) // KEY_STEP
    start = jnp.minimum(start, (total - steps * KEY_STEP) // LANES)
    return jnp.stack([start, steps - 1], -1).reshape(-1)


def head_lanes(rows, head):
    lane = lax.broadcasted_iota(jnp.int32, (rows, LANES), 1)
    return (lane >= head * HEAD_DIM) & (lane < (head + 1) * HEAD_DIM)


def only_head(array, head):
    return jnp.where(head_lanes(array.shape[0], head), array, jnp.zeros_like(array))


def folded(array, combine):
    while array.shape[0] % 16 == 0:
        half = array.shape[0] // 2
        array = combine(array[:half], array[half:])
    return array


def by_width(steps, most, branch):
    lax.switch(steps, [functools.partial(branch, (n + 1) * KEY_STEP) for n in range(most)])


def masked(scores_t, key_ids, query_ids):
    wide_ids = jnp.tile(key_ids, (1, scores_t.shape[1] // LANES))
    return jnp.where(wide_ids == query_ids, scores_t, MASKED_SCORE)


def attend_kernel(block, ranges, q_ref, k_ref, v_ref, qid_ref, kid_ref, ctx_ref, low_ref, lse_ref):
    count = q_ref.shape[1] // block
    total = k_ref.shape[1]
    base = pl.program_id(0) * count

    def one_block(index, carry):
        rows = pl.ds(pl.multiple_of(index * block, block), block)
        start = pl.multiple_of(ranges[2 * (base + index)] * LANES, LANES)
        steps = ranges[2 * (base + index) + 1]

        def branch(width):
            keys = pl.ds(start, width)
            key_part = k_ref[0, keys, :]
            value_part = v_ref[0, keys, :]
            key_ids = kid_ref[0, keys, :]
            query_ids = qid_ref[0, :, rows]
            query_part = q_ref[0, rows, :] * jnp.asarray(SCALE, LOW)
            parts = []
            for head in range(HEAD_PAIR):
                scores = times_transposed(key_part, only_head(query_part, head))
                scores = masked(scores, key_ids, query_ids)
                top = jnp.max(folded(scores, jnp.maximum), 0, keepdims=True)
                powers = jnp.exp(scores - top)
                denominator = jnp.sum(folded(powers, jnp.add), 0, keepdims=True)
                probs_low = (powers * (1.0 / denominator)).astype(LOW)
                lse_ref[0, 0, head : head + 1, rows] = top + jnp.log(denominator)
                both = transposed_times(value_part, probs_low)
                parts.append(both[head * HEAD_DIM : (head + 1) * HEAD_DIM])
            context = jnp.transpose(jnp.concatenate(parts, 0))
            ctx_ref[0, rows, :] = context
            low_ref[0, rows, :] = context.astype(LOW)

        by_width(steps, total // KEY_STEP, branch)
        return carry

    lax.fori_loop(0, count, one_block, 0)


def attend_back_kernel(
    block,
    ranges,
    q_ref,
    k_ref,
    v_ref,
    g_ref,
    ctx_ref,
    lse_ref,
    qid_ref,
    kid_ref,
    dq_ref,
    dk_ref,
    dv_ref,
    dk_sum,
    dv_sum,
):
    count = q_ref.shape[1] // block
    total = k_ref.shape[1]
    base = pl.program_id(0) * count
    dk_sum[...] = jnp.zeros_like(dk_sum)
    dv_sum[...] = jnp.zeros_like(dv_sum)

    def one_block(index, carry):
        rows = pl.ds(pl.multiple_of(index * block, block), block)
        start = pl.multiple_of(ranges[2 * (base + index)] * LANES, LANES)
        steps = ranges[2 * (base + index) + 1]

        def branch(width):
            keys = pl.ds(start, width)
            key_part = k_ref[0, keys, :]
            value_part = v_ref[0, keys, :] * jnp.asarray(SCALE, LOW)
            key_ids = kid_ref[0, keys, :]
            query_ids = qid_ref[0, :, rows]
            query_part = q_ref[0, rows, :]
            grad_part = g_ref[0, rows, :]
            products = jnp.transpose(grad_part.astype(WIDE) * ctx_ref[0, rows, :])
            dq_parts = []
            dk_total = None
            dv_total = None
            for head in range(HEAD_PAIR):
                query_head = only_head(query_part, head)
                grad_head = only_head(grad_part, head)
                scores = times_transposed(key_part, query_head * jnp.asarray(SCALE, LOW))
                scores = masked(scores, key_ids, query_ids)
                probs = jnp.exp(scores - lse_ref[0, 0, head : head + 1, rows])
                probs_low = probs.astype(LOW)
                delta = SCALE * jnp.sum(
                    products[head * HEAD_DIM : (head + 1) * HEAD_DIM], 0, keepdims=True
                )
                grad_probs = times_transposed(value_part, grad_head)
                grad_scores = (probs * (grad_probs - delta)).astype(LOW)
                dv_part = product(probs_low, grad_head)
                dk_part = product(grad_scores, query_head)
                dq_parts.append(transposed_times(grad_scores, key_part))
                dk_total = dk_part if dk_total is None else dk_total + dk_part
                dv_total = dv_part if dv_total is None else dv_total + dv_part
            dq = dq_parts[0]
            for head in range(1, HEAD_PAIR):
                dq = jnp.where(head_lanes(block, head), dq_parts[head], dq)
            dq_ref[0, rows, :] = dq.astype(LOW)
            dk_sum[keys, :] += dk_total
            dv_sum[keys, :] += dv_total

        by_width(steps, total // KEY_STEP, branch)
        return carry

    lax.fori_loop(0, count, one_block, 0)
    dk_ref[0] = dk_sum[...].astype(LOW)
    dv_ref[0] = dv_sum[...].astype(LOW)


def attention_specs(queries, keys_all, block):
    seqs, length, width = queries.shape
    total = keys_all.shape[1]
    pairs = width // LANES
    per_query = pl.BlockSpec((1, length, LANES), lambda s, h, _: (s, 0, h))
    per_key = pl.BlockSpec((1, total, LANES), lambda s, h, _: (s, 0, h))
    lse_spec = pl.BlockSpec((1, 1, HEAD_PAIR, length), lambda s, h, _: (s, h, 0, 0))
    qid_spec = pl.BlockSpec((1, 1, length), lambda s, h, _: (s, 0, 0))
    kid_spec = pl.BlockSpec((1, total, LANES), lambda s, h, _: (s, 0, 0))
    return (seqs, pairs), per_query, per_key, lse_spec, qid_spec, kid_spec


def attend(queries, keys_all, values_all, tables):
    ranges, query_ids, key_ids, block = tables
    grid, per_query, per_key, lse_spec, qid_spec, kid_spec = attention_specs(
        queries, keys_all, block
    )
    seqs, length, width = queries.shape
    return pl.pallas_call(
        functools.partial(attend_kernel, block),
        grid_spec=pltpu.PrefetchScalarGridSpec(
            num_scalar_prefetch=1,
            grid=grid,
            in_specs=[per_query, per_key, per_key, qid_spec, kid_spec],
            out_specs=[per_query, per_query, lse_spec],
        ),
        out_shape=[
            jax.ShapeDtypeStruct(queries.shape, WIDE),
            jax.ShapeDtypeStruct(queries.shape, LOW),
            jax.ShapeDtypeStruct((seqs, grid[1], HEAD_PAIR, length), WIDE),
        ],
        name="attend",
    )(ranges, queries, keys_all, values_all, query_ids, key_ids)


def attend_back(queries, keys_all, values_all, grad_context, context, lse, tables):
    ranges, query_ids, key_ids, block = tables
    grid, per_query, per_key, lse_spec, qid_spec, kid_spec = attention_specs(
        queries, keys_all, block
    )
    total = keys_all.shape[1]
    return pl.pallas_call(
        functools.partial(attend_back_kernel, block),
        grid_spec=pltpu.PrefetchScalarGridSpec(
            num_scalar_prefetch=1,
            grid=grid,
            in_specs=[
                per_query,
                per_key,
                per_key,
                per_query,
                per_query,
                lse_spec,
                qid_spec,
                kid_spec,
            ],
            out_specs=[per_query, per_key, per_key],
            scratch_shapes=[pltpu.VMEM((total, LANES), WIDE), pltpu.VMEM((total, LANES), WIDE)],
        ),
        out_shape=[
            jax.ShapeDtypeStruct(queries.shape, LOW),
            jax.ShapeDtypeStruct(keys_all.shape, LOW),
            jax.ShapeDtypeStruct(keys_all.shape, LOW),
        ],
        name="attend_back",
    )(ranges, queries, keys_all, values_all, grad_context, context, lse, query_ids, key_ids)


def exchange(pieces, ranks):
    arrived = [pieces[0]]
    for shift in range(1, ranks):
        pairs = [(i, (i + shift) % ranks) for i in range(ranks)]
        arrived.append(lax.ppermute(pieces[shift], "ctx", pairs))
    return arrived


def in_order(arrived, rank, axis):
    ranks = len(arrived)
    return jnp.concatenate(
        [lax.select_n((rank + ranks - at) % ranks, *arrived) for at in range(ranks)]
        if ranks > 2
        else [jnp.where(rank == at, arrived[0], arrived[1]) for at in range(ranks)],
        axis,
    )


def swap_in(array, ranks, rank, ready=None):
    pieces = [
        lax.dynamic_slice_in_dim(array, (rank + shift) % ranks, 1, 0) for shift in range(ranks)
    ]
    if ready is None:
        return in_order(exchange(pieces, ranks), rank, 1)
    pieces, ready = lax.optimization_barrier((pieces, ready))
    return in_order(exchange(pieces, ranks), rank, 1), ready


def swap_out(array, ranks, rank):
    part = array.shape[1] // ranks
    pieces = [
        lax.dynamic_slice_in_dim(array, (rank + shift) % ranks * part, part, 1)
        for shift in range(ranks)
    ]
    return in_order(exchange(pieces, ranks), rank, 0)


def owner_bits(dp_size, ctx_size):
    dp_bits = [("dp", at) for at in reversed(range(dp_size.bit_length() - 1))]
    return dp_bits + [("ctx", at) for at in reversed(range(ctx_size.bit_length() - 1))]


def halving_order(bits, color):
    near, far = ("dp", 0), bits[0]
    middle = [bit for bit in bits if bit not in (near, far)]
    middle.reverse()
    turn = color % max(len(middle), 1)
    return [near] + middle[turn:] + middle[:turn] + ([far] if far != near else [])


def own_bit(bit):
    axis, at = bit
    return (lax.axis_index(axis) >> at) & 1


def to_partner(array, bit):
    axis, at = bit
    return lax.ppermute(array, axis, [(i, i ^ (1 << at)) for i in range(lax.axis_size(axis))])


def taken(array, which, where):
    return lax.dynamic_index_in_dim(array, which, where, keepdims=False)


def parted(blocks, bits, color):
    bit = halving_order(bits, color)[0]
    at = bits.index(bit)
    blocks = [block.reshape((2,) * len(bits) + block.shape[1:]) for block in blocks]
    mine = [taken(block, own_bit(bit), at) for block in blocks]
    away = [taken(block, 1 - own_bit(bit), at).astype(LOW) for block in blocks]
    return mine, jnp.concatenate(away, -2)


def scatter_sum(mine, away, bits, color):
    first, *others = halving_order(bits, color)
    left = [bit for bit in bits if bit != first]
    came = to_partner(away, first)
    rows = 0
    sums = []
    for part in mine:
        more = came[..., rows : rows + part.shape[-2], :]
        sums.append((part + more.astype(WIDE)).astype(LOW))
        rows += part.shape[-2]
    total = jnp.concatenate(sums, -2)
    for bit in others:
        at = left.index(bit)
        came = to_partner(taken(total, 1 - own_bit(bit), at), bit)
        total = taken(total, own_bit(bit), at).astype(WIDE) + came.astype(WIDE)
        total = total.astype(LOW) if bit != others[-1] else total
        left.pop(at)
    return total.astype(WIDE)


def gather_all(own, bits, color):
    have = []
    for bit in reversed(halving_order(bits, color)):
        came = to_partner(own, bit)
        at = sum(bits.index(other) < bits.index(bit) for other in have)
        low, high = jnp.where(own_bit(bit) == 0, own, came), jnp.where(own_bit(bit) == 0, came, own)
        own = jnp.stack([low, high], at)
        have.append(bit)
    return own.reshape((-1,) + own.shape[len(bits) :])


def column_blocks(matrix, width):
    return [
        matrix[..., at * width : (at + 1) * width] for at in range(matrix.shape[-1] // width)
    ]


def row_blocks(matrix, count):
    rows = matrix.shape[-2] // count
    return [matrix[..., at * rows : (at + 1) * rows, :] for at in range(count)]


def vector_block(vectors, own, width):
    lines = jnp.concatenate([vector.reshape(vector.shape[:-1] + (-1, own)) for vector in vectors], -2)
    more = -lines.shape[-2] % 16
    return jnp.pad(lines, [(0, 0)] * (lines.ndim - 2) + [(0, more), (0, width - own)])


def from_vector_block(block, shards, own):
    vectors, at = [], 0
    for shard in shards:
        lines = shard.shape[0] // own
        vectors.append(block[..., at : at + lines, :own].reshape(block.shape[:-2] + (-1,)))
        at += lines
    return vectors


def body(tokens, segments, cotangent, *shards):
    matrices, vectors = shards[:6], shards[6:]
    dp_size, ranks = lax.axis_size("dp"), lax.axis_size("ctx")
    owners = dp_size * ranks
    rank = lax.axis_index("ctx")
    micro_count, local_len, width = tokens.shape
    whole_here = micro_count == ranks
    bits = owner_bits(dp_size, ranks)
    own_rows = matrices[0].shape[0]
    joined = lambda whole: whole.reshape(-1, whole.shape[-1])

    with jax.named_scope("gather"):
        later = jnp.concatenate(
            [matrices[3]] + column_blocks(matrices[4], width) + [matrices[5]], 0
        )
        later = lax.all_gather(later, ("dp", "ctx"), axis=0, tiled=False)
        sent = [matrices[0], matrices[1], jnp.concatenate([matrices[2], vector_block(vectors, own_rows, width)], 0)]
        query_mat, key_mat, last = [gather_all(own, bits, at) for at, own in enumerate(sent)]
        value_mat = joined(last[:, :own_rows])
        query_mat, key_mat = joined(query_mat), joined(key_mat)
        (
            query_bias,
            value_bias,
            output_bias,
            gain_first,
            shift_first,
            inner_bias,
            outer_bias,
            gain_second,
            shift_second,
        ) = [whole.reshape(-1).astype(WIDE) for whole in from_vector_block(last[:, own_rows:], vectors, own_rows)]
        inner_count = matrices[4].shape[1] // width
        output_mat = joined(later[:, :own_rows])
        inner_mat = jnp.concatenate(
            [
                joined(later[:, (1 + at) * own_rows : (2 + at) * own_rows])
                for at in range(inner_count)
            ],
            1,
        )
        outer_mat = joined(later[:, (1 + inner_count) * own_rows :])

    with jax.named_scope("swap_in"):
        if whole_here:
            inputs = swap_in(tokens, ranks, rank)
            doc_ids = lax.dynamic_slice_in_dim(segments, rank, 1, 0)
            own_ids = doc_ids
        else:
            inputs, doc_ids = tokens, segments
            own_ids = lax.dynamic_slice_in_dim(doc_ids, rank * local_len, local_len, 1)
    seqs, length, _ = inputs.shape
    block = min(256, length)
    tables = (
        key_ranges(own_ids, doc_ids, block),
        own_ids[:, None, :],
        jnp.broadcast_to(doc_ids[:, :, None], doc_ids.shape + (LANES,)),
        block,
    )
    by_seq = lambda array: array.reshape(seqs, -1, width)
    inputs = inputs.reshape(-1, width)

    def all_keys(own):
        own = by_seq(own)
        return own if whole_here else lax.all_gather(own, "ctx", axis=1, tiled=True)

    def own_keys(terms):
        if not whole_here:
            terms = lax.psum_scatter(terms, "ctx", scatter_dimension=1, tiled=True)
        return terms.reshape(-1, width)

    with jax.named_scope("forward"):
        queries = by_seq((product(inputs, query_mat) + query_bias).astype(LOW))
        keys_all = all_keys(product(inputs, key_mat).astype(LOW))
        values_all = all_keys((product(inputs, value_mat) + value_bias).astype(LOW))
        if whole_here:
            grad_result, queries = swap_in(cotangent, ranks, rank, queries)
        else:
            grad_result = cotangent
        grad_result = grad_result.reshape(-1, width)
        context, context_low, lse = attend(queries, keys_all, values_all, tables)
        context_low = context_low.reshape(-1, width)
        first_sum = inputs.astype(WIDE) + product(context_low, output_mat) + output_bias
        first_out, first_normed, first_rstd = layer_norm(first_sum, gain_first, shift_first)
        first_low = first_out.astype(LOW)
        inner_pre = product(first_low, inner_mat) + inner_bias
        normal_cdf, normal_pdf = normal_parts(inner_pre)
        activated = (inner_pre * normal_cdf).astype(LOW)
        second_sum = first_out + product(activated, outer_mat) + outer_bias
        result, second_normed, second_rstd = layer_norm(second_sum, gain_second, shift_second)

    with jax.named_scope("backward"):
        grad_gain_two = jnp.sum(grad_result * second_normed, 0)
        grad_shift_two = jnp.sum(grad_result, 0)
        grad_second = norm_back(grad_result, second_normed, second_rstd, gain_second)
        grad_second_low = grad_second.astype(LOW)
        grad_outer_bias = jnp.sum(grad_second, 0)
        grad_act = times_transposed(grad_second_low, outer_mat)
        grad_inner = grad_act * (normal_cdf + inner_pre * normal_pdf)
        grad_inner_low = grad_inner.astype(LOW)
        grad_inner_bias = jnp.sum(grad_inner, 0)
        grad_first_out = grad_second + times_transposed(grad_inner_low, inner_mat)
        grad_gain_one = jnp.sum(grad_first_out * first_normed, 0)
        grad_shift_one = jnp.sum(grad_first_out, 0)
        grad_first = norm_back(grad_first_out, first_normed, first_rstd, gain_first)
        grad_first_low = grad_first.astype(LOW)
        grad_output_bias = jnp.sum(grad_first, 0)
        by_owner = lambda term: term.reshape(owners, -1, term.shape[1])
        early = (
            [by_owner(transposed_times(context_low, grad_first_low))]
            + column_blocks(by_owner(transposed_times(first_low, grad_inner_low)), width)
            + row_blocks(by_owner(transposed_times(activated, grad_second_low)), inner_count)
        )
        early = jnp.concatenate([term.astype(LOW) for term in early], 1)
        grad_context = by_seq(times_transposed(grad_first_low, output_mat).astype(LOW))
        early, grad_context, result = lax.optimization_barrier((early, grad_context, result))
        early_sums = lax.psum_scatter(
            early, ("dp", "ctx"), scatter_dimension=0, tiled=False
        ).astype(WIDE)
        results = swap_out(by_seq(result), ranks, rank) if whole_here else by_seq(result)
        dq, dk, dv = attend_back(
            queries, keys_all, values_all, grad_context, context, lse, tables
        )
        dq, dk, dv, results = lax.optimization_barrier((dq, dk, dv, results))
        grad_query_low = dq.reshape(-1, width)
        grad_key_low = own_keys(dk)
        grad_value_low = own_keys(dv)
        late = [
            by_owner(transposed_times(inputs, grad_low))
            for grad_low in (grad_query_low, grad_key_low, grad_value_low)
        ]
        vector_terms = (
            jnp.sum(grad_query_low.astype(WIDE), 0),
            jnp.sum(grad_value_low.astype(WIDE), 0),
            grad_output_bias,
            grad_gain_one,
            grad_shift_one,
            grad_inner_bias,
            grad_outer_bias,
            grad_gain_two,
            grad_shift_two,
        )
        lines = vector_block([term.reshape(owners, -1) for term in vector_terms], own_rows, width)
        mine, away = zip(parted(late[:2], bits, 0), parted([late[2], lines], bits, 1))
        away, grad_query_low, grad_key_low, grad_value_low = lax.optimization_barrier(
            (away, grad_query_low, grad_key_low, grad_value_low)
        )
        late_sums = [scatter_sum(mine[at], away[at], bits, at) for at in range(len(away))]
        input_grad = (
            grad_first
            + times_transposed(grad_query_low, query_mat)
            + times_transposed(grad_key_low, key_mat)
            + times_transposed(grad_value_low, value_mat)
        )

    with jax.named_scope("owned"):
        rows = row_blocks(early_sums, early_sums.shape[0] // own_rows)
        own_lines = late_sums[1][own_rows:]
        owned_grads = [
            late_sums[0][:own_rows],
            late_sums[0][own_rows:],
            late_sums[1][:own_rows],
            rows[0],
            jnp.concatenate(rows[1 : 1 + inner_count], 1),
            jnp.concatenate(rows[1 + inner_count :], 0),
        ] + from_vector_block(own_lines, vectors, own_rows)

    with jax.named_scope("swap_out"):
        if whole_here:
            input_grads = swap_out(by_seq(input_grad).astype(LOW), ranks, rank).astype(WIDE)
        else:
            input_grads = by_seq(input_grad)
    return (results, input_grads) + tuple(owned_grads)


def solution(mesh):
    by_tokens = P("dp", "ctx", None)
    matrix = P(("dp", "ctx"), None)
    vector = P(("dp", "ctx"))
    grads = (matrix,) * 6 + (vector,) * 9
    in_specs = (by_tokens, P("dp", None), by_tokens) + grads
    out_specs = (by_tokens, by_tokens) + grads
    return jax.shard_map(body, mesh=mesh, in_specs=in_specs, out_specs=out_specs, check_vma=False)
```

```python
import functools

import jax
import jax.numpy as jnp
from jax import lax
from jax.experimental import pallas as pl
from jax.experimental.pallas import tpu as pltpu
from jax.sharding import PartitionSpec as P

HEAD_DIM = 64
EPSILON = 1e-12
MASKED_SCORE = -1e30
LANES = 128
HEAD_PAIR = LANES // HEAD_DIM
SCALE = HEAD_DIM**-0.5
KEY_STEP = 256
GROUP = 2
ATTEND_BLOCK = 512
ATTEND_BACK_BLOCK = 256

WIDE = jnp.float32
LOW = jnp.bfloat16


def product(left_side, right_side):
    return jnp.dot(left_side, right_side, preferred_element_type=WIDE)


def times_transposed(left_side, right_side):
    return lax.dot_general(
        left_side, right_side, (((1,), (1,)), ((), ())), preferred_element_type=WIDE
    )


def transposed_times(left_side, right_side):
    return lax.dot_general(
        left_side, right_side, (((0,), (0,)), ((), ())), preferred_element_type=WIDE
    )


def layer_norm(summed, gain_vec, shift_vec):
    row_mean = jnp.mean(summed, -1, keepdims=True)
    centred = summed - row_mean
    variance = jnp.mean(centred * centred, -1, keepdims=True)
    inv_std = lax.rsqrt(variance + EPSILON)
    normed = centred * inv_std
    return (normed * gain_vec + shift_vec, normed, inv_std)


def norm_back(upstream, normed, inv_std, gain_vec):
    scaled_grad = upstream * gain_vec
    first_term = jnp.mean(scaled_grad, -1, keepdims=True)
    second_term = jnp.mean(scaled_grad * normed, -1, keepdims=True)
    return inv_std * (scaled_grad - first_term - normed * second_term)


def normal_parts(inner_pre):
    normal_cdf = 0.5 * (1.0 + lax.erf(inner_pre * 0.7071067811865476))
    normal_pdf = jnp.exp(-0.5 * inner_pre * inner_pre) * 0.3989422804014327
    return (normal_cdf, normal_pdf)


def key_ranges(own_ids, doc_ids, block):
    total = doc_ids.shape[-1]
    blocks = own_ids.reshape(own_ids.shape[0], -1, block)
    first = blocks[:, :, 0]
    last = blocks[:, :, -1]
    begin = jnp.sum(doc_ids[:, None, :] < first[:, :, None], -1, dtype=jnp.int32)
    end = jnp.sum(doc_ids[:, None, :] <= last[:, :, None], -1, dtype=jnp.int32)
    start = begin // LANES
    steps = (end - start * LANES + KEY_STEP - 1) // KEY_STEP
    start = jnp.minimum(start, (total - steps * KEY_STEP) // LANES)
    return jnp.stack([start, steps - 1], -1).reshape(-1)


def head_lanes(rows, head):
    lane = lax.broadcasted_iota(jnp.int32, (rows, LANES), 1)
    return (lane >= head * HEAD_DIM) & (lane < (head + 1) * HEAD_DIM)


def only_head(array, head):
    return jnp.where(head_lanes(array.shape[0], head), array, jnp.zeros_like(array))


def folded(array, combine):
    while array.shape[0] % 16 == 0:
        half = array.shape[0] // 2
        array = combine(array[:half], array[half:])
    return array


def by_width(steps, most, branch):
    lax.switch(steps, [functools.partial(branch, (n + 1) * KEY_STEP) for n in range(most)])


def masked(scores_t, key_ids, query_ids):
    wide_ids = jnp.tile(key_ids, (1, scores_t.shape[1] // LANES))
    return jnp.where(wide_ids == query_ids, scores_t, MASKED_SCORE)


def attend_kernel(block, ranges, q_ref, k_ref, v_ref, qid_ref, kid_ref, ctx_ref, low_ref, lse_ref):
    count = q_ref.shape[1] // block
    total = k_ref.shape[1]
    base = pl.program_id(0) * count

    def one_block(index, carry):
        rows = pl.ds(pl.multiple_of(index * block, block), block)
        start = pl.multiple_of(ranges[2 * (base + index)] * LANES, LANES)
        steps = ranges[2 * (base + index) + 1]

        def branch(width):
            keys = pl.ds(start, width)
            key_ids = kid_ref[0, keys, :]
            query_ids = qid_ref[0, :, rows]
            for pair in range(q_ref.shape[2] // LANES):
                lanes = slice(pair * LANES, (pair + 1) * LANES)
                key_part = k_ref[0, keys, lanes]
                value_part = v_ref[0, keys, lanes]
                query_part = q_ref[0, rows, lanes] * jnp.asarray(SCALE, LOW)
                parts = []
                for head in range(HEAD_PAIR):
                    scores = times_transposed(key_part, only_head(query_part, head))
                    scores = masked(scores, key_ids, query_ids)
                    top = jnp.max(folded(scores, jnp.maximum), 0, keepdims=True)
                    powers = jnp.exp(scores - top)
                    denominator = jnp.sum(folded(powers, jnp.add), 0, keepdims=True)
                    probs_low = (powers * (1.0 / denominator)).astype(LOW)
                    lse_ref[0, pair, head : head + 1, rows] = top + jnp.log(denominator)
                    both = transposed_times(value_part, probs_low)
                    parts.append(both[head * HEAD_DIM : (head + 1) * HEAD_DIM])
                context = jnp.transpose(jnp.concatenate(parts, 0))
                ctx_ref[0, rows, lanes] = context
                low_ref[0, rows, lanes] = context.astype(LOW)

        by_width(steps, total // KEY_STEP, branch)
        return carry

    lax.fori_loop(0, count, one_block, 0)


def attend_back_kernel(
    block,
    ranges,
    q_ref,
    k_ref,
    v_ref,
    g_ref,
    ctx_ref,
    lse_ref,
    qid_ref,
    kid_ref,
    dq_ref,
    dk_ref,
    dv_ref,
    dk_sum,
    dv_sum,
):
    count = q_ref.shape[1] // block
    total = k_ref.shape[1]
    base = pl.program_id(0) * count
    dk_sum[...] = jnp.zeros_like(dk_sum)
    dv_sum[...] = jnp.zeros_like(dv_sum)

    def one_block(index, carry):
        rows = pl.ds(pl.multiple_of(index * block, block), block)
        start = pl.multiple_of(ranges[2 * (base + index)] * LANES, LANES)
        steps = ranges[2 * (base + index) + 1]

        def branch(width):
            keys = pl.ds(start, width)
            key_ids = kid_ref[0, keys, :]
            query_ids = qid_ref[0, :, rows]
            for pair in range(q_ref.shape[2] // LANES):
                lanes = slice(pair * LANES, (pair + 1) * LANES)
                key_part = k_ref[0, keys, lanes]
                value_part = v_ref[0, keys, lanes] * jnp.asarray(SCALE, LOW)
                query_part = q_ref[0, rows, lanes]
                grad_part = g_ref[0, rows, lanes]
                products = jnp.transpose(grad_part.astype(WIDE) * ctx_ref[0, rows, lanes])
                dq_parts = []
                dk_total = None
                dv_total = None
                for head in range(HEAD_PAIR):
                    query_head = only_head(query_part, head)
                    grad_head = only_head(grad_part, head)
                    scores = times_transposed(key_part, query_head * jnp.asarray(SCALE, LOW))
                    scores = masked(scores, key_ids, query_ids)
                    probs = jnp.exp(scores - lse_ref[0, pair, head : head + 1, rows])
                    probs_low = probs.astype(LOW)
                    delta = SCALE * jnp.sum(
                        products[head * HEAD_DIM : (head + 1) * HEAD_DIM], 0, keepdims=True
                    )
                    grad_probs = times_transposed(value_part, grad_head)
                    grad_scores = (probs * (grad_probs - delta)).astype(LOW)
                    dv_part = product(probs_low, grad_head)
                    dk_part = product(grad_scores, query_head)
                    dq_parts.append(transposed_times(grad_scores, key_part))
                    dk_total = dk_part if dk_total is None else dk_total + dk_part
                    dv_total = dv_part if dv_total is None else dv_total + dv_part
                dq = dq_parts[0]
                for head in range(1, HEAD_PAIR):
                    dq = jnp.where(head_lanes(block, head), dq_parts[head], dq)
                dq_ref[0, rows, lanes] = dq.astype(LOW)
                dk_sum[keys, lanes] += dk_total
                dv_sum[keys, lanes] += dv_total

        by_width(steps, total // KEY_STEP, branch)
        return carry

    lax.fori_loop(0, count, one_block, 0)
    dk_ref[0] = dk_sum[...].astype(LOW)
    dv_ref[0] = dv_sum[...].astype(LOW)


def attention_specs(queries, keys_all, block):
    seqs, length, width = queries.shape
    total = keys_all.shape[1]
    pairs = width // LANES
    group = GROUP if pairs % GROUP == 0 else 1
    per_query = pl.BlockSpec((1, length, group * LANES), lambda s, h, _: (s, 0, h))
    per_key = pl.BlockSpec((1, total, group * LANES), lambda s, h, _: (s, 0, h))
    lse_spec = pl.BlockSpec((1, group, HEAD_PAIR, length), lambda s, h, _: (s, h, 0, 0))
    qid_spec = pl.BlockSpec((1, 1, length), lambda s, h, _: (s, 0, 0))
    kid_spec = pl.BlockSpec((1, total, LANES), lambda s, h, _: (s, 0, 0))
    return (seqs, pairs // group), per_query, per_key, lse_spec, qid_spec, kid_spec


def attend(queries, keys_all, values_all, tables):
    ranges, query_ids, key_ids, block = tables
    grid, per_query, per_key, lse_spec, qid_spec, kid_spec = attention_specs(
        queries, keys_all, block
    )
    seqs, length, width = queries.shape
    return pl.pallas_call(
        functools.partial(attend_kernel, block),
        grid_spec=pltpu.PrefetchScalarGridSpec(
            num_scalar_prefetch=1,
            grid=grid,
            in_specs=[per_query, per_key, per_key, qid_spec, kid_spec],
            out_specs=[per_query, per_query, lse_spec],
        ),
        out_shape=[
            jax.ShapeDtypeStruct(queries.shape, WIDE),
            jax.ShapeDtypeStruct(queries.shape, LOW),
            jax.ShapeDtypeStruct((seqs, width // LANES, HEAD_PAIR, length), WIDE),
        ],
        name="attend",
    )(ranges, queries, keys_all, values_all, query_ids, key_ids)


def attend_back(queries, keys_all, values_all, grad_context, context, lse, tables):
    ranges, query_ids, key_ids, block = tables
    grid, per_query, per_key, lse_spec, qid_spec, kid_spec = attention_specs(
        queries, keys_all, block
    )
    total = keys_all.shape[1]
    return pl.pallas_call(
        functools.partial(attend_back_kernel, block),
        grid_spec=pltpu.PrefetchScalarGridSpec(
            num_scalar_prefetch=1,
            grid=grid,
            in_specs=[
                per_query,
                per_key,
                per_key,
                per_query,
                per_query,
                lse_spec,
                qid_spec,
                kid_spec,
            ],
            out_specs=[per_query, per_key, per_key],
            scratch_shapes=[
                pltpu.VMEM((total, per_key.block_shape[2]), WIDE),
                pltpu.VMEM((total, per_key.block_shape[2]), WIDE),
            ],
        ),
        out_shape=[
            jax.ShapeDtypeStruct(queries.shape, LOW),
            jax.ShapeDtypeStruct(keys_all.shape, LOW),
            jax.ShapeDtypeStruct(keys_all.shape, LOW),
        ],
        name="attend_back",
    )(ranges, queries, keys_all, values_all, grad_context, context, lse, query_ids, key_ids)


def exchange(pieces, ranks):
    arrived = [pieces[0]]
    for shift in range(1, ranks):
        pairs = [(i, (i + shift) % ranks) for i in range(ranks)]
        arrived.append(lax.ppermute(pieces[shift], "ctx", pairs))
    return arrived


def in_order(arrived, rank, axis):
    ranks = len(arrived)
    return jnp.concatenate(
        [lax.select_n((rank + ranks - at) % ranks, *arrived) for at in range(ranks)]
        if ranks > 2
        else [jnp.where(rank == at, arrived[0], arrived[1]) for at in range(ranks)],
        axis,
    )


def swap_in(array, ranks, rank, ready=None):
    if ready is not None:
        rank, ready = lax.optimization_barrier((rank, ready))
    pieces = [
        lax.dynamic_slice_in_dim(array, (rank + shift) % ranks, 1, 0) for shift in range(ranks)
    ]
    whole = in_order(exchange(pieces, ranks), rank, 1)
    return whole if ready is None else (whole, ready)


def swap_out(array, ranks, rank):
    part = array.shape[1] // ranks
    pieces = [
        lax.dynamic_slice_in_dim(array, (rank + shift) % ranks * part, part, 1)
        for shift in range(ranks)
    ]
    return in_order(exchange(pieces, ranks), rank, 0)


def owner_bits(dp_size, ctx_size):
    dp_bits = [("dp", at) for at in reversed(range(dp_size.bit_length() - 1))]
    return dp_bits + [("ctx", at) for at in reversed(range(ctx_size.bit_length() - 1))]


def halving_order(bits, color):
    near, far = ("dp", 0), bits[0]
    middle = [bit for bit in bits if bit not in (near, far)]
    middle.reverse()
    turn = color % max(len(middle), 1)
    return [near] + middle[turn:] + middle[:turn] + ([far] if far != near else [])


def own_bit(bit):
    axis, at = bit
    return (lax.axis_index(axis) >> at) & 1


def to_partner(array, bit):
    axis, at = bit
    return lax.ppermute(array, axis, [(i, i ^ (1 << at)) for i in range(lax.axis_size(axis))])


def taken(array, which, where):
    return lax.dynamic_index_in_dim(array, which, where, keepdims=False)


def parted(blocks, bits, color):
    bit = halving_order(bits, color)[0]
    at = bits.index(bit)
    blocks = [block.reshape((2,) * len(bits) + block.shape[1:]) for block in blocks]
    mine = [taken(block, own_bit(bit), at) for block in blocks]
    away = [taken(block, 1 - own_bit(bit), at).astype(LOW) for block in blocks]
    return mine, jnp.concatenate(away, -2)


def scatter_sum(mine, away, bits, color):
    first, *others = halving_order(bits, color)
    left = [bit for bit in bits if bit != first]
    came = to_partner(away, first)
    rows = 0
    sums = []
    for part in mine:
        more = came[..., rows : rows + part.shape[-2], :]
        sums.append((part + more.astype(WIDE)).astype(LOW))
        rows += part.shape[-2]
    total = jnp.concatenate(sums, -2)
    for bit in others:
        at = left.index(bit)
        came = to_partner(taken(total, 1 - own_bit(bit), at), bit)
        total = taken(total, own_bit(bit), at).astype(WIDE) + came.astype(WIDE)
        total = total.astype(LOW) if bit != others[-1] else total
        left.pop(at)
    return total.astype(WIDE)


def gather_all(own, bits, color):
    have = []
    for bit in reversed(halving_order(bits, color)):
        came = to_partner(own, bit)
        at = sum(bits.index(other) < bits.index(bit) for other in have)
        low, high = jnp.where(own_bit(bit) == 0, own, came), jnp.where(own_bit(bit) == 0, came, own)
        own = jnp.stack([low, high], at)
        have.append(bit)
    return own.reshape((-1,) + own.shape[len(bits) :])


def column_blocks(matrix, width):
    return [
        matrix[..., at * width : (at + 1) * width] for at in range(matrix.shape[-1] // width)
    ]


def row_blocks(matrix, count):
    rows = matrix.shape[-2] // count
    return [matrix[..., at * rows : (at + 1) * rows, :] for at in range(count)]


def vector_block(vectors, own, width):
    lines = jnp.concatenate([vector.reshape(vector.shape[:-1] + (-1, own)) for vector in vectors], -2)
    more = -lines.shape[-2] % 16
    return jnp.pad(lines, [(0, 0)] * (lines.ndim - 2) + [(0, more), (0, width - own)])


def from_vector_block(block, shards, own):
    vectors, at = [], 0
    for shard in shards:
        lines = shard.shape[0] // own
        vectors.append(block[..., at : at + lines, :own].reshape(block.shape[:-2] + (-1,)))
        at += lines
    return vectors


def body(tokens, segments, cotangent, *shards):
    matrices, vectors = shards[:6], shards[6:]
    dp_size, ranks = lax.axis_size("dp"), lax.axis_size("ctx")
    owners = dp_size * ranks
    rank = lax.axis_index("ctx")
    micro_count, local_len, width = tokens.shape
    whole_here = micro_count == ranks
    bits = owner_bits(dp_size, ranks)
    own_rows = matrices[0].shape[0]
    joined = lambda whole: whole.reshape(-1, whole.shape[-1])

    with jax.named_scope("gather"):
        later = jnp.concatenate(
            [matrices[3]] + column_blocks(matrices[4], width) + [matrices[5]], 0
        )
        later = lax.all_gather(later, ("dp", "ctx"), axis=0, tiled=False)
        sent = [matrices[0], matrices[1], jnp.concatenate([matrices[2], vector_block(vectors, own_rows, width)], 0)]
        query_mat, key_mat, last = [gather_all(own, bits, at) for at, own in enumerate(sent)]
        value_mat = joined(last[:, :own_rows])
        query_mat, key_mat = joined(query_mat), joined(key_mat)
        (
            query_bias,
            value_bias,
            output_bias,
            gain_first,
            shift_first,
            inner_bias,
            outer_bias,
            gain_second,
            shift_second,
        ) = [whole.reshape(-1).astype(WIDE) for whole in from_vector_block(last[:, own_rows:], vectors, own_rows)]
        inner_count = matrices[4].shape[1] // width
        output_mat = joined(later[:, :own_rows])
        inner_mat = jnp.concatenate(
            [
                joined(later[:, (1 + at) * own_rows : (2 + at) * own_rows])
                for at in range(inner_count)
            ],
            1,
        )
        outer_mat = joined(later[:, (1 + inner_count) * own_rows :])

    with jax.named_scope("swap_in"):
        if whole_here:
            inputs = swap_in(tokens, ranks, rank)
            doc_ids = lax.dynamic_slice_in_dim(segments, rank, 1, 0)
            own_ids = doc_ids
        else:
            inputs, doc_ids = tokens, segments
            own_ids = lax.dynamic_slice_in_dim(doc_ids, rank * local_len, local_len, 1)
    seqs, length, _ = inputs.shape
    query_ids = own_ids[:, None, :]
    key_ids = jnp.broadcast_to(doc_ids[:, :, None], doc_ids.shape + (LANES,))
    tables, back_tables = [
        (key_ranges(own_ids, doc_ids, block), query_ids, key_ids, block)
        for block in (min(ATTEND_BLOCK, length), min(ATTEND_BACK_BLOCK, length))
    ]
    by_seq = lambda array: array.reshape(seqs, -1, width)
    inputs = inputs.reshape(-1, width)

    def all_keys(own):
        own = by_seq(own)
        return own if whole_here else lax.all_gather(own, "ctx", axis=1, tiled=True)

    def own_keys(terms):
        if not whole_here:
            terms = lax.psum_scatter(terms, "ctx", scatter_dimension=1, tiled=True)
        return terms.reshape(-1, width)

    with jax.named_scope("forward"):
        queries = by_seq((product(inputs, query_mat) + query_bias).astype(LOW))
        keys_all = all_keys(product(inputs, key_mat).astype(LOW))
        values_all = all_keys((product(inputs, value_mat) + value_bias).astype(LOW))
        if whole_here:
            grad_result, queries = swap_in(cotangent, ranks, rank, queries)
        else:
            grad_result = cotangent
        grad_result = grad_result.reshape(-1, width)
        context, context_low, lse = attend(queries, keys_all, values_all, tables)
        context_low = context_low.reshape(-1, width)
        first_sum = inputs.astype(WIDE) + product(context_low, output_mat) + output_bias
        first_out, first_normed, first_rstd = layer_norm(first_sum, gain_first, shift_first)
        first_low = first_out.astype(LOW)
        inner_pre = product(first_low, inner_mat) + inner_bias
        normal_cdf, normal_pdf = normal_parts(inner_pre)
        activated = (inner_pre * normal_cdf).astype(LOW)
        second_sum = first_out + product(activated, outer_mat) + outer_bias
        result, second_normed, second_rstd = layer_norm(second_sum, gain_second, shift_second)

    with jax.named_scope("backward"):
        grad_gain_two = jnp.sum(grad_result * second_normed, 0)
        grad_shift_two = jnp.sum(grad_result, 0)
        grad_second = norm_back(grad_result, second_normed, second_rstd, gain_second)
        grad_second_low = grad_second.astype(LOW)
        grad_outer_bias = jnp.sum(grad_second, 0)
        grad_act = times_transposed(grad_second_low, outer_mat)
        grad_inner = grad_act * (normal_cdf + inner_pre * normal_pdf)
        grad_inner_low = grad_inner.astype(LOW)
        grad_inner_bias = jnp.sum(grad_inner, 0)
        grad_first_out = grad_second + times_transposed(grad_inner_low, inner_mat)
        grad_gain_one = jnp.sum(grad_first_out * first_normed, 0)
        grad_shift_one = jnp.sum(grad_first_out, 0)
        grad_first = norm_back(grad_first_out, first_normed, first_rstd, gain_first)
        grad_first_low = grad_first.astype(LOW)
        grad_output_bias = jnp.sum(grad_first, 0)
        by_owner = lambda term: term.reshape(owners, -1, term.shape[1])
        early = (
            [by_owner(transposed_times(context_low, grad_first_low))]
            + column_blocks(by_owner(transposed_times(first_low, grad_inner_low)), width)
            + row_blocks(by_owner(transposed_times(activated, grad_second_low)), inner_count)
        )
        early = jnp.concatenate([term.astype(LOW) for term in early], 1)
        grad_context = by_seq(times_transposed(grad_first_low, output_mat).astype(LOW))
        early, grad_context, result = lax.optimization_barrier((early, grad_context, result))
        early_sums = lax.psum_scatter(
            early, ("dp", "ctx"), scatter_dimension=0, tiled=False
        ).astype(WIDE)
        results = swap_out(by_seq(result), ranks, rank) if whole_here else by_seq(result)
        dq, dk, dv = attend_back(
            queries, keys_all, values_all, grad_context, context, lse, back_tables
        )
        dq, dk, dv, results = lax.optimization_barrier((dq, dk, dv, results))
        grad_query_low = dq.reshape(-1, width)
        grad_key_low = own_keys(dk)
        grad_value_low = own_keys(dv)
        late = [
            by_owner(transposed_times(inputs, grad_low))
            for grad_low in (grad_query_low, grad_key_low, grad_value_low)
        ]
        vector_terms = (
            jnp.sum(grad_query_low.astype(WIDE), 0),
            jnp.sum(grad_value_low.astype(WIDE), 0),
            grad_output_bias,
            grad_gain_one,
            grad_shift_one,
            grad_inner_bias,
            grad_outer_bias,
            grad_gain_two,
            grad_shift_two,
        )
        lines = vector_block([term.reshape(owners, -1) for term in vector_terms], own_rows, width)
        mine, away = zip(parted(late[:2], bits, 0), parted([late[2], lines], bits, 1))
        away, grad_query_low, grad_key_low, grad_value_low = lax.optimization_barrier(
            (away, grad_query_low, grad_key_low, grad_value_low)
        )
        late_sums = [scatter_sum(mine[at], away[at], bits, at) for at in range(len(away))]
        input_grad = (
            grad_first
            + times_transposed(grad_query_low, query_mat)
            + times_transposed(grad_key_low, key_mat)
            + times_transposed(grad_value_low, value_mat)
        )

    with jax.named_scope("owned"):
        rows = row_blocks(early_sums, early_sums.shape[0] // own_rows)
        own_lines = late_sums[1][own_rows:]
        owned_grads = [
            late_sums[0][:own_rows],
            late_sums[0][own_rows:],
            late_sums[1][:own_rows],
            rows[0],
            jnp.concatenate(rows[1 : 1 + inner_count], 1),
            jnp.concatenate(rows[1 + inner_count :], 0),
        ] + from_vector_block(own_lines, vectors, own_rows)

    with jax.named_scope("swap_out"):
        if whole_here:
            input_grads = swap_out(by_seq(input_grad).astype(LOW), ranks, rank).astype(WIDE)
        else:
            input_grads = by_seq(input_grad)
    return (results, input_grads) + tuple(owned_grads)


def solution(mesh):
    by_tokens = P("dp", "ctx", None)
    matrix = P(("dp", "ctx"), None)
    vector = P(("dp", "ctx"))
    grads = (matrix,) * 6 + (vector,) * 9
    in_specs = (by_tokens, P("dp", None), by_tokens) + grads
    out_specs = (by_tokens, by_tokens) + grads
    return jax.shard_map(body, mesh=mesh, in_specs=in_specs, out_specs=out_specs, check_vma=False)
```

```python
import functools

import jax
import jax.numpy as jnp
from jax import lax
from jax.experimental import pallas as pl
from jax.experimental.pallas import tpu as pltpu
from jax.sharding import PartitionSpec as P

HEAD_DIM = 64
EPSILON = 1e-12
MASKED_SCORE = -1e30
LANES = 128
HEAD_PAIR = LANES // HEAD_DIM
SCALE = HEAD_DIM**-0.5
KEY_STEP = 256
GROUP = 2
ATTEND_BLOCK = 512
ATTEND_BACK_BLOCK = 256

WIDE = jnp.float32
LOW = jnp.bfloat16


def product(left_side, right_side):
    return jnp.dot(left_side, right_side, preferred_element_type=WIDE)


def times_transposed(left_side, right_side):
    return lax.dot_general(
        left_side, right_side, (((1,), (1,)), ((), ())), preferred_element_type=WIDE
    )


def transposed_times(left_side, right_side):
    return lax.dot_general(
        left_side, right_side, (((0,), (0,)), ((), ())), preferred_element_type=WIDE
    )


def layer_norm(summed, gain_vec, shift_vec):
    row_mean = jnp.mean(summed, -1, keepdims=True)
    centred = summed - row_mean
    variance = jnp.mean(centred * centred, -1, keepdims=True)
    inv_std = lax.rsqrt(variance + EPSILON)
    normed = centred * inv_std
    return (normed * gain_vec + shift_vec, normed, inv_std)


def norm_back(upstream, normed, inv_std, gain_vec):
    scaled_grad = upstream * gain_vec
    first_term = jnp.mean(scaled_grad, -1, keepdims=True)
    second_term = jnp.mean(scaled_grad * normed, -1, keepdims=True)
    return inv_std * (scaled_grad - first_term - normed * second_term)


def normal_parts(inner_pre):
    normal_cdf = 0.5 * (1.0 + lax.erf(inner_pre * 0.7071067811865476))
    normal_pdf = jnp.exp(-0.5 * inner_pre * inner_pre) * 0.3989422804014327
    return (normal_cdf, normal_pdf)


def key_ranges(own_ids, doc_ids, block):
    total = doc_ids.shape[-1]
    blocks = own_ids.reshape(own_ids.shape[0], -1, block)
    first = blocks[:, :, 0]
    last = blocks[:, :, -1]
    begin = jnp.sum(doc_ids[:, None, :] < first[:, :, None], -1, dtype=jnp.int32)
    end = jnp.sum(doc_ids[:, None, :] <= last[:, :, None], -1, dtype=jnp.int32)
    start = begin // LANES
    steps = (end - start * LANES + KEY_STEP - 1) // KEY_STEP
    start = jnp.minimum(start, (total - steps * KEY_STEP) // LANES)
    return jnp.stack([start, steps - 1], -1).reshape(-1)


def head_lanes(rows, head):
    lane = lax.broadcasted_iota(jnp.int32, (rows, LANES), 1)
    return (lane >= head * HEAD_DIM) & (lane < (head + 1) * HEAD_DIM)


def only_head(array, head):
    return jnp.where(head_lanes(array.shape[0], head), array, jnp.zeros_like(array))


def folded(array, combine):
    while array.shape[0] % 16 == 0:
        half = array.shape[0] // 2
        array = combine(array[:half], array[half:])
    return array


def by_width(steps, most, branch):
    lax.switch(steps, [functools.partial(branch, (n + 1) * KEY_STEP) for n in range(most)])


def masked(scores_t, key_ids, query_ids):
    wide_ids = jnp.tile(key_ids, (1, scores_t.shape[1] // LANES))
    return jnp.where(wide_ids == query_ids, scores_t, MASKED_SCORE)


def attend_kernel(block, ranges, q_ref, k_ref, v_ref, qid_ref, kid_ref, ctx_ref, low_ref, lse_ref):
    count = q_ref.shape[1] // block
    total = k_ref.shape[1]
    base = pl.program_id(0) * count

    def one_block(index, carry):
        rows = pl.ds(pl.multiple_of(index * block, block), block)
        start = pl.multiple_of(ranges[2 * (base + index)] * LANES, LANES)
        steps = ranges[2 * (base + index) + 1]

        def branch(width):
            keys = pl.ds(start, width)
            key_ids = kid_ref[0, keys, :]
            query_ids = qid_ref[0, :, rows]
            for pair in range(q_ref.shape[2] // LANES):
                lanes = slice(pair * LANES, (pair + 1) * LANES)
                key_part = k_ref[0, keys, lanes]
                value_part = v_ref[0, keys, lanes]
                query_part = q_ref[0, rows, lanes] * jnp.asarray(SCALE, LOW)
                parts = []
                for head in range(HEAD_PAIR):
                    scores = times_transposed(key_part, only_head(query_part, head))
                    scores = masked(scores, key_ids, query_ids)
                    top = jnp.max(folded(scores, jnp.maximum), 0, keepdims=True)
                    powers = jnp.exp(scores - top)
                    denominator = jnp.sum(folded(powers, jnp.add), 0, keepdims=True)
                    probs_low = (powers * (1.0 / denominator)).astype(LOW)
                    lse_ref[0, pair, head : head + 1, rows] = top + jnp.log(denominator)
                    both = transposed_times(value_part, probs_low)
                    parts.append(both[head * HEAD_DIM : (head + 1) * HEAD_DIM])
                context = jnp.transpose(jnp.concatenate(parts, 0))
                ctx_ref[0, rows, lanes] = context
                low_ref[0, rows, lanes] = context.astype(LOW)

        by_width(steps, total // KEY_STEP, branch)
        return carry

    lax.fori_loop(0, count, one_block, 0)


def attend_back_kernel(
    block,
    ranges,
    q_ref,
    k_ref,
    v_ref,
    g_ref,
    ctx_ref,
    lse_ref,
    qid_ref,
    kid_ref,
    dq_ref,
    dk_ref,
    dv_ref,
    dk_sum,
    dv_sum,
):
    count = q_ref.shape[1] // block
    total = k_ref.shape[1]
    base = pl.program_id(0) * count
    dk_sum[...] = jnp.zeros_like(dk_sum)
    dv_sum[...] = jnp.zeros_like(dv_sum)

    def one_block(index, carry):
        rows = pl.ds(pl.multiple_of(index * block, block), block)
        start = pl.multiple_of(ranges[2 * (base + index)] * LANES, LANES)
        steps = ranges[2 * (base + index) + 1]

        def branch(width):
            keys = pl.ds(start, width)
            key_ids = kid_ref[0, keys, :]
            query_ids = qid_ref[0, :, rows]
            for pair in range(q_ref.shape[2] // LANES):
                lanes = slice(pair * LANES, (pair + 1) * LANES)
                key_part = k_ref[0, keys, lanes]
                value_part = v_ref[0, keys, lanes] * jnp.asarray(SCALE, LOW)
                query_part = q_ref[0, rows, lanes]
                grad_part = g_ref[0, rows, lanes]
                products = jnp.transpose(grad_part.astype(WIDE) * ctx_ref[0, rows, lanes])
                dq_parts = []
                dk_total = None
                dv_total = None
                for head in range(HEAD_PAIR):
                    query_head = only_head(query_part, head)
                    grad_head = only_head(grad_part, head)
                    scores = times_transposed(key_part, query_head * jnp.asarray(SCALE, LOW))
                    scores = masked(scores, key_ids, query_ids)
                    probs = jnp.exp(scores - lse_ref[0, pair, head : head + 1, rows])
                    probs_low = probs.astype(LOW)
                    delta = SCALE * jnp.sum(
                        products[head * HEAD_DIM : (head + 1) * HEAD_DIM], 0, keepdims=True
                    )
                    grad_probs = times_transposed(value_part, grad_head)
                    grad_scores = (probs * (grad_probs - delta)).astype(LOW)
                    dv_part = product(probs_low, grad_head)
                    dk_part = product(grad_scores, query_head)
                    dq_parts.append(transposed_times(grad_scores, key_part))
                    dk_total = dk_part if dk_total is None else dk_total + dk_part
                    dv_total = dv_part if dv_total is None else dv_total + dv_part
                dq = dq_parts[0]
                for head in range(1, HEAD_PAIR):
                    dq = jnp.where(head_lanes(block, head), dq_parts[head], dq)
                dq_ref[0, rows, lanes] = dq.astype(LOW)
                dk_sum[keys, lanes] += dk_total
                dv_sum[keys, lanes] += dv_total

        by_width(steps, total // KEY_STEP, branch)
        return carry

    lax.fori_loop(0, count, one_block, 0)
    dk_ref[0] = dk_sum[...].astype(LOW)
    dv_ref[0] = dv_sum[...].astype(LOW)


def attention_specs(queries, keys_all, block):
    seqs, length, width = queries.shape
    total = keys_all.shape[1]
    pairs = width // LANES
    group = GROUP if pairs % GROUP == 0 else 1
    per_query = pl.BlockSpec((1, length, group * LANES), lambda s, h, _: (s, 0, h))
    per_key = pl.BlockSpec((1, total, group * LANES), lambda s, h, _: (s, 0, h))
    lse_spec = pl.BlockSpec((1, group, HEAD_PAIR, length), lambda s, h, _: (s, h, 0, 0))
    qid_spec = pl.BlockSpec((1, 1, length), lambda s, h, _: (s, 0, 0))
    kid_spec = pl.BlockSpec((1, total, LANES), lambda s, h, _: (s, 0, 0))
    return (seqs, pairs // group), per_query, per_key, lse_spec, qid_spec, kid_spec


def attend(queries, keys_all, values_all, tables):
    ranges, query_ids, key_ids, block = tables
    grid, per_query, per_key, lse_spec, qid_spec, kid_spec = attention_specs(
        queries, keys_all, block
    )
    seqs, length, width = queries.shape
    return pl.pallas_call(
        functools.partial(attend_kernel, block),
        grid_spec=pltpu.PrefetchScalarGridSpec(
            num_scalar_prefetch=1,
            grid=grid,
            in_specs=[per_query, per_key, per_key, qid_spec, kid_spec],
            out_specs=[per_query, per_query, lse_spec],
        ),
        out_shape=[
            jax.ShapeDtypeStruct(queries.shape, WIDE),
            jax.ShapeDtypeStruct(queries.shape, LOW),
            jax.ShapeDtypeStruct((seqs, width // LANES, HEAD_PAIR, length), WIDE),
        ],
        name="attend",
    )(ranges, queries, keys_all, values_all, query_ids, key_ids)


def attend_back(queries, keys_all, values_all, grad_context, context, lse, tables):
    ranges, query_ids, key_ids, block = tables
    grid, per_query, per_key, lse_spec, qid_spec, kid_spec = attention_specs(
        queries, keys_all, block
    )
    total = keys_all.shape[1]
    return pl.pallas_call(
        functools.partial(attend_back_kernel, block),
        grid_spec=pltpu.PrefetchScalarGridSpec(
            num_scalar_prefetch=1,
            grid=grid,
            in_specs=[
                per_query,
                per_key,
                per_key,
                per_query,
                per_query,
                lse_spec,
                qid_spec,
                kid_spec,
            ],
            out_specs=[per_query, per_key, per_key],
            scratch_shapes=[
                pltpu.VMEM((total, per_key.block_shape[2]), WIDE),
                pltpu.VMEM((total, per_key.block_shape[2]), WIDE),
            ],
        ),
        out_shape=[
            jax.ShapeDtypeStruct(queries.shape, LOW),
            jax.ShapeDtypeStruct(keys_all.shape, LOW),
            jax.ShapeDtypeStruct(keys_all.shape, LOW),
        ],
        name="attend_back",
    )(ranges, queries, keys_all, values_all, grad_context, context, lse, query_ids, key_ids)


def exchange(pieces, ranks):
    arrived = [pieces[0]]
    for shift in range(1, ranks):
        pairs = [(i, (i + shift) % ranks) for i in range(ranks)]
        arrived.append(lax.ppermute(pieces[shift], "ctx", pairs))
    return arrived


def in_order(arrived, rank, axis):
    ranks = len(arrived)
    return jnp.concatenate(
        [lax.select_n((rank + ranks - at) % ranks, *arrived) for at in range(ranks)]
        if ranks > 2
        else [jnp.where(rank == at, arrived[0], arrived[1]) for at in range(ranks)],
        axis,
    )


def swap_in(array, ranks, rank, ready=None):
    if ready is not None:
        rank, ready = lax.optimization_barrier((rank, ready))
    pieces = [
        lax.dynamic_slice_in_dim(array, (rank + shift) % ranks, 1, 0) for shift in range(ranks)
    ]
    whole = in_order(exchange(pieces, ranks), rank, 1)
    return whole if ready is None else (whole, ready)


def swap_out(array, ranks, rank):
    part = array.shape[1] // ranks
    pieces = [
        lax.dynamic_slice_in_dim(array, (rank + shift) % ranks * part, part, 1)
        for shift in range(ranks)
    ]
    return in_order(exchange(pieces, ranks), rank, 0)


def owner_bits(dp_size, ctx_size):
    dp_bits = [("dp", at) for at in reversed(range(dp_size.bit_length() - 1))]
    return dp_bits + [("ctx", at) for at in reversed(range(ctx_size.bit_length() - 1))]


def halving_order(bits, color):
    near, far = ("dp", 0), bits[0]
    middle = [bit for bit in bits if bit not in (near, far)]
    middle.reverse()
    turn = color % max(len(middle), 1)
    return [near] + middle[turn:] + middle[:turn] + ([far] if far != near else [])


def own_bit(bit):
    axis, at = bit
    return (lax.axis_index(axis) >> at) & 1


def to_partner(array, bit):
    axis, at = bit
    return lax.ppermute(array, axis, [(i, i ^ (1 << at)) for i in range(lax.axis_size(axis))])


def taken(array, which, where):
    return lax.dynamic_index_in_dim(array, which, where, keepdims=False)


def parted(blocks, bits, color):
    bit = halving_order(bits, color)[0]
    at = bits.index(bit)
    blocks = [block.reshape((2,) * len(bits) + block.shape[1:]) for block in blocks]
    mine = [taken(block, own_bit(bit), at) for block in blocks]
    away = [taken(block, 1 - own_bit(bit), at).astype(LOW) for block in blocks]
    return mine, jnp.concatenate(away, -2)


def scatter_sum(mine, away, bits, color):
    first, *others = halving_order(bits, color)
    left = [bit for bit in bits if bit != first]
    came = to_partner(away, first)
    rows = 0
    sums = []
    for part in mine:
        more = came[..., rows : rows + part.shape[-2], :]
        sums.append((part + more.astype(WIDE)).astype(LOW))
        rows += part.shape[-2]
    total = jnp.concatenate(sums, -2)
    for bit in others:
        at = left.index(bit)
        came = to_partner(taken(total, 1 - own_bit(bit), at), bit)
        total = taken(total, own_bit(bit), at).astype(WIDE) + came.astype(WIDE)
        total = total.astype(LOW) if bit != others[-1] else total
        left.pop(at)
    return total.astype(WIDE)


def gather_all(own, bits, color):
    have = []
    for bit in reversed(halving_order(bits, color)):
        came = to_partner(own, bit)
        at = sum(bits.index(other) < bits.index(bit) for other in have)
        low, high = jnp.where(own_bit(bit) == 0, own, came), jnp.where(own_bit(bit) == 0, came, own)
        own = jnp.stack([low, high], at)
        have.append(bit)
    return own.reshape((-1,) + own.shape[len(bits) :])


def column_blocks(matrix, width):
    return [
        matrix[..., at * width : (at + 1) * width] for at in range(matrix.shape[-1] // width)
    ]


def row_blocks(matrix, count):
    rows = matrix.shape[-2] // count
    return [matrix[..., at * rows : (at + 1) * rows, :] for at in range(count)]


def vector_block(vectors, own, width):
    lines = jnp.concatenate([vector.reshape(vector.shape[:-1] + (-1, own)) for vector in vectors], -2)
    more = -lines.shape[-2] % 16
    return jnp.pad(lines, [(0, 0)] * (lines.ndim - 2) + [(0, more), (0, width - own)])


def from_vector_block(block, shards, own):
    vectors, at = [], 0
    for shard in shards:
        lines = shard.shape[0] // own
        vectors.append(block[..., at : at + lines, :own].reshape(block.shape[:-2] + (-1,)))
        at += lines
    return vectors


def body(tokens, segments, cotangent, *shards):
    matrices, vectors = shards[:6], shards[6:]
    dp_size, ranks = lax.axis_size("dp"), lax.axis_size("ctx")
    owners = dp_size * ranks
    rank = lax.axis_index("ctx")
    micro_count, local_len, width = tokens.shape
    whole_here = micro_count == ranks
    bits = owner_bits(dp_size, ranks)
    own_rows = matrices[0].shape[0]
    joined = lambda whole: whole.reshape(-1, whole.shape[-1])

    with jax.named_scope("gather"):
        later = jnp.concatenate(
            [matrices[3]] + column_blocks(matrices[4], width) + [matrices[5]], 0
        )
        later = lax.all_gather(later, ("dp", "ctx"), axis=0, tiled=False)
        sent = [matrices[0], matrices[1], jnp.concatenate([matrices[2], vector_block(vectors, own_rows, width)], 0)]
        query_mat, key_mat, last = [gather_all(own, bits, at) for at, own in enumerate(sent)]
        value_mat = joined(last[:, :own_rows])
        query_mat, key_mat = joined(query_mat), joined(key_mat)
        (
            query_bias,
            value_bias,
            output_bias,
            gain_first,
            shift_first,
            inner_bias,
            outer_bias,
            gain_second,
            shift_second,
        ) = [whole.reshape(-1).astype(WIDE) for whole in from_vector_block(last[:, own_rows:], vectors, own_rows)]
        inner_count = matrices[4].shape[1] // width
        output_mat = joined(later[:, :own_rows])
        inner_mat = jnp.concatenate(
            [
                joined(later[:, (1 + at) * own_rows : (2 + at) * own_rows])
                for at in range(inner_count)
            ],
            1,
        )
        outer_mat = joined(later[:, (1 + inner_count) * own_rows :])

    with jax.named_scope("swap_in"):
        if whole_here:
            inputs = swap_in(tokens, ranks, rank)
            doc_ids = lax.dynamic_slice_in_dim(segments, rank, 1, 0)
            own_ids = doc_ids
        else:
            inputs, doc_ids = tokens, segments
            own_ids = lax.dynamic_slice_in_dim(doc_ids, rank * local_len, local_len, 1)
    seqs, length, _ = inputs.shape
    query_ids = own_ids[:, None, :]
    key_ids = jnp.broadcast_to(doc_ids[:, :, None], doc_ids.shape + (LANES,))
    tables, back_tables = [
        (key_ranges(own_ids, doc_ids, block), query_ids, key_ids, block)
        for block in (min(ATTEND_BLOCK, length), min(ATTEND_BACK_BLOCK, length))
    ]
    by_seq = lambda array: array.reshape(seqs, -1, width)
    inputs = inputs.reshape(-1, width)

    def all_keys(own):
        own = by_seq(own)
        return own if whole_here else lax.all_gather(own, "ctx", axis=1, tiled=True)

    def own_keys(terms):
        if not whole_here:
            terms = lax.psum_scatter(terms, "ctx", scatter_dimension=1, tiled=True)
        return terms.reshape(-1, width)

    with jax.named_scope("forward"):
        queries = by_seq((product(inputs, query_mat) + query_bias).astype(LOW))
        keys_all = all_keys(product(inputs, key_mat).astype(LOW))
        values_all = all_keys((product(inputs, value_mat) + value_bias).astype(LOW))
        if whole_here:
            grad_result, queries = swap_in(cotangent, ranks, rank, queries)
        else:
            grad_result = cotangent
        grad_result = grad_result.reshape(-1, width)
        context, context_low, lse = attend(queries, keys_all, values_all, tables)
        context_low = context_low.reshape(-1, width)
        first_sum = inputs.astype(WIDE) + product(context_low, output_mat) + output_bias
        first_out, first_normed, first_rstd = layer_norm(first_sum, gain_first, shift_first)
        first_low = first_out.astype(LOW)
        inner_pre = product(first_low, inner_mat) + inner_bias
        normal_cdf, normal_pdf = normal_parts(inner_pre)
        activated = (inner_pre * normal_cdf).astype(LOW)
        second_sum = first_out + product(activated, outer_mat) + outer_bias
        result, second_normed, second_rstd = layer_norm(second_sum, gain_second, shift_second)

    with jax.named_scope("backward"):
        grad_gain_two = jnp.sum(grad_result * second_normed, 0)
        grad_shift_two = jnp.sum(grad_result, 0)
        grad_second = norm_back(grad_result, second_normed, second_rstd, gain_second)
        grad_second_low = grad_second.astype(LOW)
        grad_outer_bias = jnp.sum(grad_second, 0)
        grad_act = times_transposed(grad_second_low, outer_mat)
        grad_inner = grad_act * (normal_cdf + inner_pre * normal_pdf)
        grad_inner_low = grad_inner.astype(LOW)
        grad_inner_bias = jnp.sum(grad_inner, 0)
        grad_first_out = grad_second + times_transposed(grad_inner_low, inner_mat)
        grad_gain_one = jnp.sum(grad_first_out * first_normed, 0)
        grad_shift_one = jnp.sum(grad_first_out, 0)
        grad_first = norm_back(grad_first_out, first_normed, first_rstd, gain_first)
        grad_first_low = grad_first.astype(LOW)
        grad_output_bias = jnp.sum(grad_first, 0)
        by_owner = lambda term: term.reshape(owners, -1, term.shape[1])
        early = (
            [by_owner(transposed_times(context_low, grad_first_low))]
            + column_blocks(by_owner(transposed_times(first_low, grad_inner_low)), width)
            + row_blocks(by_owner(transposed_times(activated, grad_second_low)), inner_count)
        )
        early = jnp.concatenate([term.astype(LOW) for term in early], 1)
        early, grad_first_low, result = lax.optimization_barrier((early, grad_first_low, result))
        grad_context = by_seq(times_transposed(grad_first_low, output_mat).astype(LOW))
        early_sums = lax.psum_scatter(
            early, ("dp", "ctx"), scatter_dimension=0, tiled=False
        ).astype(WIDE)
        results = swap_out(by_seq(result), ranks, rank) if whole_here else by_seq(result)
        dq, dk, dv = attend_back(
            queries, keys_all, values_all, grad_context, context, lse, back_tables
        )
        dq, dk, dv, results = lax.optimization_barrier((dq, dk, dv, results))
        grad_query_low = dq.reshape(-1, width)
        grad_key_low = own_keys(dk)
        grad_value_low = own_keys(dv)
        late = [
            by_owner(transposed_times(inputs, grad_low))
            for grad_low in (grad_query_low, grad_key_low, grad_value_low)
        ]
        vector_terms = (
            jnp.sum(grad_query_low.astype(WIDE), 0),
            jnp.sum(grad_value_low.astype(WIDE), 0),
            grad_output_bias,
            grad_gain_one,
            grad_shift_one,
            grad_inner_bias,
            grad_outer_bias,
            grad_gain_two,
            grad_shift_two,
        )
        lines = vector_block([term.reshape(owners, -1) for term in vector_terms], own_rows, width)
        mine, away = zip(parted(late[:2], bits, 0), parted([late[2], lines], bits, 1))
        away, grad_query_low, grad_key_low, grad_value_low = lax.optimization_barrier(
            (away, grad_query_low, grad_key_low, grad_value_low)
        )
        late_sums = [scatter_sum(mine[at], away[at], bits, at) for at in range(len(away))]
        input_grad = (
            grad_first
            + times_transposed(grad_query_low, query_mat)
            + times_transposed(grad_key_low, key_mat)
            + times_transposed(grad_value_low, value_mat)
        )

    with jax.named_scope("owned"):
        rows = row_blocks(early_sums, early_sums.shape[0] // own_rows)
        own_lines = late_sums[1][own_rows:]
        owned_grads = [
            late_sums[0][:own_rows],
            late_sums[0][own_rows:],
            late_sums[1][:own_rows],
            rows[0],
            jnp.concatenate(rows[1 : 1 + inner_count], 1),
            jnp.concatenate(rows[1 + inner_count :], 0),
        ] + from_vector_block(own_lines, vectors, own_rows)

    with jax.named_scope("swap_out"):
        if whole_here:
            input_grads = swap_out(by_seq(input_grad).astype(LOW), ranks, rank).astype(WIDE)
        else:
            input_grads = by_seq(input_grad)
    return (results, input_grads) + tuple(owned_grads)


def solution(mesh):
    by_tokens = P("dp", "ctx", None)
    matrix = P(("dp", "ctx"), None)
    vector = P(("dp", "ctx"))
    grads = (matrix,) * 6 + (vector,) * 9
    in_specs = (by_tokens, P("dp", None), by_tokens) + grads
    out_specs = (by_tokens, by_tokens) + grads
    return jax.shard_map(body, mesh=mesh, in_specs=in_specs, out_specs=out_specs, check_vma=False)
```
